256 devices in a mesh: section: 4 (over y_hi, core), ctx: 16 (over y_lo, z), tp: 4 (over x).
Axes of the slice: x: 4, y: 4 (y_hi: 2, y_lo: 2; y = y_hi * 2 + y_lo), z: 8, core: 2. Of those that a mesh axis runs over, the one named last changes fastest.
Arguments:
- mixer_input: bfloat16 [4, 8192, 8192], P('section', 'ctx', 'tp'), may hold values from -6 to 6
- write_vectors: bfloat16 [4, 8192, 1024], P('section', 'ctx', 'tp'), may hold values from -6 to 6
- read_vectors: bfloat16 [4, 8192, 1024], P('section', 'ctx', 'tp'), may hold values from -6 to 6
- delta_raw: float32 [4, 8192, 128], P('section', 'ctx', 'tp'), as said below
- log_rates: float32 [4, 128], P('section', 'tp'), as said below
- delta_bias: float32 [4, 128], P('section', 'tp'), as said below
- skip_gain: float32 [4, 128], P('section', 'tp'), may hold values from 0.5 to 1.5
- output_grad: bfloat16 [4, 8192, 8192], P('section', 'ctx', 'tp'), may hold values from -6 to 6
Outputs:
- upstream_grad: bfloat16 [4, 8192, 8192], P('section', 'ctx', 'tp')
- grad_delta: float32 [4, 8192, 128], P('section', 'ctx', 'tp')
- grad_vectors: float32 [4, 8192, 2048], P('section', ('ctx', 'tp'))
- grad_params: float32 [4, 3, 128], P('section', None, 'tp')
The draws below stay inside these ranges and needn't reach their ends.
Inputs may be any that keep to these rules, and one draw needn't show every extreme that they name: `log_rates`: one value a head and section. `delta_bias`: one value a head and section. `delta_raw`: real-valued logits.
All inputs are finite; a program needn't handle non-finite values.
Results may differ from the reference program's by a relative error of at most 0.00365.
Values may be sent and summed in bfloat16 or wider, within the bound.
No kernel may reach another device: no remote copies, remote signals or barrier semaphores. Data moves between devices by JAX's collectives and lax.ppermute only.
A program may use at most 128 MiB of HBM per device.

```python
import jax
import jax.numpy as jnp
from jax import lax

HEADS = 128
HEADDIM = 64
STATE = 128
GROUPS = 8
BLOCK = 256
TOK_DEV = 512
TOKENS = 8192
SECTIONS = 4


def head_table(key):
    class_key = jax.random.fold_in(key, 101)
    level_key = jax.random.fold_in(key, 102)
    rate_key = jax.random.fold_in(key, 103)
    share = 0.5
    fast_heads = jax.random.uniform(class_key, (SECTIONS, HEADS), jnp.float32) < share
    level = jnp.exp(jax.random.uniform(level_key, (SECTIONS, HEADS), jnp.float32, -0.2, 0.2))
    slow_step = level / jnp.sqrt(STATE * TOKENS * 1.0)
    fast_step = 0.16 * level / jnp.sqrt(STATE * 1.0)
    base_step = jnp.where(fast_heads, fast_step, slow_step)
    spread = jax.random.uniform(rate_key, (SECTIONS, HEADS), jnp.float32, 0.0, 1.0)
    fast_rate = jnp.exp(0.25 * (2.0 * spread - 1.0)) / (40.0 * base_step)
    slow_rate = (0.3 + 0.5 * spread) / (TOKENS * base_step)
    return (base_step, jnp.where(fast_heads, fast_rate, slow_rate))


def draw_log_rates(key, part):
    base_step, rates = head_table(key)
    return jnp.log(rates)


def draw_delta_bias(key, part):
    base_step, rates = head_table(key)
    return jnp.log(jnp.expm1(base_step))


def draw_delta_raw(key, part):
    noise_key = jax.random.fold_in(key, 3)
    shift_key = jax.random.fold_in(key, 5)
    noise = 0.5 * jax.random.truncated_normal(noise_key, -2.5, 2.5, (SECTIONS, TOKENS, HEADS), jnp.float32)
    block_count = TOKENS // TOK_DEV
    offset = jax.random.uniform(shift_key, (SECTIONS, block_count, 1, HEADS), jnp.float32, -8.0, 0.7)
    offset = jnp.broadcast_to(offset, (SECTIONS, block_count, TOK_DEV, HEADS)).reshape(SECTIONS, TOKENS, HEADS)
    return noise + offset


def shard_levels(stream_key, dims, pieces, least, top_value):
    gain = 1.0
    for position, blocks in pieces:
        steps = jax.random.uniform(jax.random.fold_in(jax.random.fold_in(stream_key, 6), position), (blocks,), jnp.float32, least / len(pieces), top_value / len(pieces))
        gain = gain * jnp.repeat(jnp.exp(steps), dims[position] // blocks).reshape((-1,) + (1,) * (len(dims) - 1 - position))
    return gain


def gaussian(stream_key, dims, width, reach, pieces=(), dtype=jnp.bfloat16):
    result = jax.random.normal(stream_key, dims, jnp.float32) * width
    if len(pieces) > 0:
        result = shard_levels(stream_key, dims, pieces, -0.22, 0.18) * result
    return jnp.clip(result, min=-reach, max=reach).astype(dtype)


def setup_inputs(seed: int = 0) -> dict:
    seeds = jax.random.split(jax.random.key(seed), 9)
    return {
        "mixer_input": gaussian(seeds[0], (SECTIONS, TOKENS, HEADS * HEADDIM), 1.0, 6.0, ((0, 4), (1, 16), (2, 4))),
        "write_vectors": gaussian(seeds[1], (SECTIONS, TOKENS, GROUPS * STATE), 1.0, 6.0, ((0, 4), (1, 16), (2, 4))),
        "read_vectors": gaussian(seeds[2], (SECTIONS, TOKENS, GROUPS * STATE), 1.0, 6.0, ((0, 4), (1, 16), (2, 4))),
        "delta_raw": draw_delta_raw(jax.random.fold_in(seeds[8], 71), 0),
        "log_rates": draw_log_rates(jax.random.fold_in(seeds[8], 71), 0),
        "delta_bias": draw_delta_bias(jax.random.fold_in(seeds[8], 71), 0),
        "skip_gain": jnp.clip(0.5 + 1.0 * jax.random.uniform(seeds[6], (SECTIONS, HEADS), jnp.float32) ** shard_levels(seeds[6], (SECTIONS, HEADS), ((0, 4), (1, 4)), -0.2, 0.2), 0.5, 1.5),
        "output_grad": gaussian(seeds[7], (SECTIONS, TOKENS, HEADS * HEADDIM), 1.0, 6.0, ((0, 4), (1, 16), (2, 4))),
    }


HIGHEST = lax.Precision.HIGHEST

def block_pass(values_all, write_rows, read_rows, step_size, decay_rates, start_state):
    length, group_count, per_group, head_width = values_all.shape
    block_count = length // BLOCK
    positions = jnp.arange(BLOCK)
    causal = positions[:, None] >= positions[None, :]

    def advance(carry_state, block_item):
        values, write_block, read_block, step_rows = block_item
        cum_log = jnp.cumsum(-step_rows * decay_rates[None], axis=0)
        gap_logs = cum_log[:, None] - cum_log[None, :]
        decay_mat = jnp.exp(jnp.where(causal[:, :, None, None], gap_logs, -1e+30))
        scores = jnp.einsum('ign,jgn->ijg', read_block, write_block, precision=HIGHEST)
        weights = scores[:, :, :, None] * decay_mat * step_rows[None]
        within = jnp.einsum('ijgk,jgkp->igkp', weights, values, precision=HIGHEST)
        carried = jnp.einsum('ign,gkpn->igkp', read_block, carry_state, precision=HIGHEST)
        outputs = within + jnp.exp(cum_log)[..., None] * carried
        tail_w = jnp.exp(cum_log[-1][None] - cum_log) * step_rows
        written = jnp.einsum('jgkp,jgn->gkpn', tail_w[..., None] * values, write_block, precision=HIGHEST)
        new_state = jnp.exp(cum_log[-1])[..., None, None] * carry_state + written
        return (new_state, outputs)
    blocks_in = (values_all.reshape(block_count, BLOCK, group_count, per_group, head_width), write_rows.reshape(block_count, BLOCK, group_count, -1), read_rows.reshape(block_count, BLOCK, group_count, -1), step_size.reshape(block_count, BLOCK, group_count, per_group))
    last_state, outputs = lax.scan(jax.checkpoint(advance), start_state, blocks_in)
    return (outputs.reshape(length, group_count, per_group, head_width), last_state)

def layer_output(input_rows, write_rows, read_rows, delta_rows, rate_logs, bias_terms, skip_terms):
    length = input_rows.shape[0]
    group_count = write_rows.shape[1] // STATE
    head_count = rate_logs.shape[0]
    per_group = head_count // group_count
    step_size = jax.nn.softplus(delta_rows + bias_terms[None, :]).reshape(length, group_count, per_group)
    decay_rates = jnp.exp(rate_logs).reshape(group_count, per_group)
    values = input_rows.reshape(length, group_count, per_group, HEADDIM)
    start_state = jnp.zeros((group_count, per_group, HEADDIM, STATE), jnp.float32)
    outputs, unused = block_pass(values, write_rows.reshape(length, group_count, STATE), read_rows.reshape(length, group_count, STATE), step_size, decay_rates, start_state)
    outputs = outputs + skip_terms.reshape(group_count, per_group)[None, :, :, None] * values
    return outputs.reshape(input_rows.shape)

def reference(mixer_input, write_vectors, read_vectors, delta_raw, log_rates, delta_bias, skip_gain, output_grad):

    def one_section(section_items):
        input_rows, write_rows, read_rows, delta_rows, rate_logs, bias_terms, skip_terms, grad_rows = section_items
        unused, pullback = jax.vjp(layer_output, input_rows.astype(jnp.float32), write_rows.astype(jnp.float32), read_rows.astype(jnp.float32), delta_rows, rate_logs, bias_terms, skip_terms)
        return pullback(grad_rows.astype(jnp.float32))
    gradients = lax.map(one_section, (mixer_input, write_vectors, read_vectors, delta_raw, log_rates, delta_bias, skip_gain, output_grad))
    grad_input = gradients[0].astype(jnp.bfloat16)
    upstream = jnp.concatenate([grad_input[1:], jnp.zeros_like(grad_input[:1])], axis=0)
    section_count = gradients[1].shape[0]
    length = gradients[1].shape[1]
    grad_write = gradients[1].reshape(section_count, length, GROUPS, STATE)
    grad_read = gradients[2].reshape(section_count, length, GROUPS, STATE)
    grad_vectors = jnp.stack([grad_write, grad_read], axis=3).reshape(section_count, length, GROUPS * 2 * STATE)
    grad_params = jnp.stack([gradients[4], gradients[5], gradients[6]], axis=1)
    return (upstream, gradients[3], grad_vectors, grad_params)
```

```python
import functools

import jax
import jax.numpy as jnp
from jax import lax
from jax.experimental import pallas as pl
from jax.experimental.pallas import tpu as pltpu
from jax.sharding import PartitionSpec as P

HEADDIM = 64
STATE = 128
CHUNK = 128
LANES = 128
F32 = jnp.float32
BF16 = jnp.bfloat16
TAIL = 16


def iota(shape, dim):
    return lax.broadcasted_iota(jnp.int32, shape, dim)


def mm(a, b):
    return lax.dot_general(a, b, (((1,), (0,)), ((), ())), preferred_element_type=F32)


def mm_nt(a, b):
    return lax.dot_general(a, b, (((1,), (1,)), ((), ())), preferred_element_type=F32)


def split2(v):
    hi = v.astype(BF16)
    return hi, (v - hi.astype(F32)).astype(BF16)


def split3(v):
    hi = v.astype(BF16)
    rest = v - hi.astype(F32)
    mid = rest.astype(BF16)
    return hi, mid, (rest - mid.astype(F32)).astype(BF16)


def softplus(z):
    u = jnp.exp(-jnp.abs(z))
    small = u * (1.0 - u * (0.5 - u * (1.0 / 3.0 - u * (0.25 - u * 0.2))))
    return jnp.maximum(z, 0.0) + jnp.where(u < 0.03, small, jnp.log(1.0 + u))


def chunk_rows(c):
    return slice(c * CHUNK, (c + 1) * CHUNK)


def expand(split, pair, heads):
    depth = split.shape[1]
    row, col = iota((depth, 2 * LANES), 0), iota((depth, 2 * LANES), 1)
    kind = (row % (2 * heads)) // heads
    head = row % heads
    hit = (kind == col // LANES) & (head == 2 * pair + (col % LANES) // HEADDIM)
    out = mm(split, jnp.where(hit, 1.0, 0.0).astype(BF16))
    return out[:, :LANES], out[:, LANES:]


def head_sum(product, pair, offset):
    hi, lo = split2(product)
    row, col = iota((2 * LANES, LANES), 0), iota((2 * LANES, LANES), 1)
    hit = col == offset + 2 * pair + (row % LANES) // HEADDIM
    return mm(jnp.concatenate([hi, lo], axis=1), jnp.where(hit, 1.0, 0.0).astype(BF16))


def prep_kernel(
    x_ref, dy_ref, w_ref, r_ref, delta_ref, rate_ref, bias_ref, pay_ref, cs_ref, ct_ref, wt_ref, rt_ref,
    *, per_group
):
    pair = pl.program_id(0)
    length = x_ref.shape[0]
    heads = delta_ref.shape[1]
    chunks = length // CHUNK

    @pl.when(pair == 0)
    def _():
        step = softplus(delta_ref[...] + bias_ref[...])
        logs = jnp.maximum(jnp.log(step), -200.0)
        decay = -step * jnp.exp(rate_ref[...])
        lower = jnp.where(iota((CHUNK, CHUNK), 0) >= iota((CHUNK, CHUNK), 1), 1.0, 0.0).astype(BF16)
        for c in range(chunks):
            hi, mid, lo = split3(decay[chunk_rows(c)])
            cum = mm(lower, hi) + mm(lower, mid) + mm(lower, lo)
            both = jnp.concatenate([cum, cum - logs[chunk_rows(c)]], axis=1)
            cs_ref[chunk_rows(c), :] = jnp.concatenate(split3(both), axis=1)
            ct_ref[c] = both.T

    @pl.when(pair % per_group == 0)
    def _():
        wt_ref[...] = w_ref[...].astype(F32).T.astype(BF16)
        rt_ref[...] = r_ref[...].astype(F32).T.astype(BF16)

    cl, ll = expand(cs_ref[...], pair, heads)
    state = jnp.zeros((STATE, LANES), F32)
    total = jnp.zeros((1, LANES), F32)
    for c in range(chunks):
        rows = chunk_rows(c)
        end = cl[(c + 1) * CHUNK - 1 : (c + 1) * CHUNK]
        hi, lo = split2(x_ref[rows].astype(F32) * jnp.exp(end - ll[rows]))
        w_t = wt_ref[:, rows]
        state = jnp.exp(end) * state + mm(jnp.concatenate([w_t, w_t], 1), jnp.concatenate([hi, lo], 0))
        total = total + end
    grad = jnp.zeros((STATE, LANES), F32)
    for c in reversed(range(chunks)):
        rows = chunk_rows(c)
        end = cl[(c + 1) * CHUNK - 1 : (c + 1) * CHUNK]
        hi, lo = split2(dy_ref[rows].astype(F32) * jnp.exp(cl[rows]))
        r_t = rt_ref[:, rows]
        grad = jnp.exp(end) * grad + mm(jnp.concatenate([r_t, r_t], 1), jnp.concatenate([hi, lo], 0))
    pay_ref[0, :STATE] = state.astype(BF16)
    pay_ref[0, STATE : 2 * STATE] = grad.astype(BF16)
    carry = jnp.exp(total)
    carry_hi = carry.astype(BF16).astype(F32)
    picked = jnp.where(iota((TAIL, LANES), 0) == 0, carry_hi, carry - carry_hi)
    pay_ref[0, 2 * STATE :] = picked.astype(BF16)


def scan_kernel(in_ref, out_ref):
    places = in_ref.shape[0]

    def carry(c):
        tail = in_ref[c, 2 * STATE :].astype(F32)
        return tail[0:1] + tail[1:2]

    state = jnp.zeros((STATE, LANES), F32)
    for c in range(places):
        out_ref[c, :STATE] = state.astype(BF16)
        state = carry(c) * state + in_ref[c, :STATE].astype(F32)
    grad = jnp.zeros((STATE, LANES), F32)
    for c in reversed(range(places)):
        out_ref[c, STATE:] = grad.astype(BF16)
        grad = carry(c) * grad + in_ref[c, STATE : 2 * STATE].astype(F32)


def intra_kernel(
    x_ref, dy_ref, w_ref, r_ref, cs_ref, ct_ref, skip_ref, dxi_ref, vp_ref, dwr_ref, gsk_ref,
    sc_ref, sct_ref, dsc_ref, *, first_pair, heads
):
    place = pl.program_id(0)
    pair = first_pair + place
    length = x_ref.shape[0]
    chunks = length // CHUNK

    @pl.when(place == 0)
    def _():
        for c in range(chunks):
            rows = chunk_rows(c)
            sc_ref[c] = mm_nt(r_ref[rows], w_ref[rows])
            sct_ref[c] = mm_nt(w_ref[rows], r_ref[rows])
        dsc_ref[...] = jnp.zeros_like(dsc_ref)
        vp_ref[...] = jnp.zeros_like(vp_ref)

    cl, ll = expand(cs_ref[...], pair, heads)
    row, col = iota((CHUNK, CHUNK), 0), iota((CHUNK, CHUNK), 1)
    left = iota((CHUNK, LANES), 1) < HEADDIM
    left_b = jnp.where(left, 1.0, 0.0).astype(BF16)
    right_b = jnp.where(left, 0.0, 1.0).astype(BF16)
    skip_sum = jnp.zeros((1, LANES), F32)
    for c in range(chunks):
        rows = chunk_rows(c)
        x, dy = x_ref[rows], dy_ref[rows]
        x_two = jnp.concatenate([x * left_b, x * right_b], axis=0)
        dy_two = jnp.concatenate([dy * left_b, dy * right_b], axis=0)
        gram = mm_nt(dy, x_two)
        mixes, mixes_t = [], []
        total = dsc_ref[c]
        for k in range(2):
            lane = slice(k * HEADDIM, k * HEADDIM + 1)
            log_row = ct_ref[c, pl.ds(heads + 2 * pair + k, 1), :]
            gap = jnp.where(row >= col, cl[rows, lane] - log_row, -1e30)
            decay = jnp.exp(gap)
            mixes.append((sc_ref[c] * decay).astype(BF16))
            total = total + gram[:, k * CHUNK : (k + 1) * CHUNK] * decay
            cum_row = ct_ref[c, pl.ds(2 * pair + k, 1), :]
            gap_t = jnp.where(col >= row, cum_row - ll[rows, lane], -1e30)
            mixes_t.append((sct_ref[c] * jnp.exp(gap_t)).astype(BF16))
        dsc_ref[c] = total
        y = mm(jnp.concatenate(mixes, axis=1), x_two)
        dx = mm(jnp.concatenate(mixes_t, axis=1), dy_two)
        xf, dyf = x.astype(F32), dy.astype(F32)
        pulled = xf * dx
        vp_ref[rows] += head_sum(dyf * y - pulled, pair, 0) + head_sum(pulled, pair, 2 * heads)
        dxi_ref[rows] = dx + skip_ref[...] * dyf
        skip_sum = skip_sum + jnp.sum(xf * dyf, axis=0, keepdims=True)
    gsk_ref[pl.ds(place, 1), :] = skip_sum

    @pl.when(place == pl.num_programs(0) - 1)
    def _():
        for c in range(chunks):
            rows = chunk_rows(c)
            w, r = w_ref[rows], r_ref[rows]
            total = dsc_ref[c]
            hi, lo = split2(total)
            dwr_ref[rows, STATE:] = mm(jnp.concatenate([hi, lo], 1), jnp.concatenate([w, w], 0))
            hi, lo = split2(total.T)
            dwr_ref[rows, :STATE] = mm(jnp.concatenate([hi, lo], 1), jnp.concatenate([r, r], 0))


def inter_kernel(
    x_ref, dy_ref, w_ref, r_ref, wt_ref, rt_ref, cs_ref, st_ref, dxi_ref, vp_in_ref, dwr_in_ref,
    up_ref, vp_ref, dwr_ref, states_ref, *, first_pair, heads
):
    place = pl.program_id(0)
    pair = first_pair + place
    length = x_ref.shape[0]
    chunks = length // CHUNK

    @pl.when(place == 0)
    def _():
        vp_ref[...] = vp_in_ref[...]
        dwr_ref[...] = dwr_in_ref[...]

    cl, ll = expand(cs_ref[...], pair, heads)
    last = iota((CHUNK, LANES), 0) == CHUNK - 1
    state = st_ref[0, :STATE].astype(F32)
    for c in range(chunks):
        rows = chunk_rows(c)
        states_ref[c] = state
        end = cl[(c + 1) * CHUNK - 1 : (c + 1) * CHUNK]
        tail = jnp.exp(end - ll[rows])
        hi, lo = split2(x_ref[rows].astype(F32) * tail)
        w_t = wt_ref[:, rows]
        state = jnp.exp(end) * state + mm(jnp.concatenate([w_t, w_t], 1), jnp.concatenate([hi, lo], 0))
    states_ref[chunks] = state
    grad = st_ref[0, STATE:].astype(F32)
    for c in reversed(range(chunks)):
        rows = chunk_rows(c)
        end = cl[(c + 1) * CHUNK - 1 : (c + 1) * CHUNK]
        w, r = w_ref[rows], r_ref[rows]
        xf, dyf = x_ref[rows].astype(F32), dy_ref[rows].astype(F32)
        tail = jnp.exp(end - ll[rows])
        seen = jnp.exp(cl[rows])
        s_hi, s_lo = split2(states_ref[c])
        g_hi, g_lo = split2(grad)
        y = seen * mm(jnp.concatenate([r, r], 1), jnp.concatenate([s_hi, s_lo], 0))
        dx = tail * mm(jnp.concatenate([w, w], 1), jnp.concatenate([g_hi, g_lo], 0))
        edge = jnp.sum(states_ref[c + 1] * grad, axis=0, keepdims=True)
        pulled = xf * dx
        push = dyf * y - pulled + jnp.where(last, edge, 0.0)
        vp_ref[rows] += head_sum(push, pair, 0) + head_sum(pulled, pair, 2 * heads)
        up_ref[rows] = (dxi_ref[rows] + dx).astype(BF16)
        d_hi, d_lo = split2(dyf * seen)
        x_hi, x_lo = split2(xf * tail)
        dwr_ref[rows, :STATE] += mm_nt(
            jnp.concatenate([x_hi, x_lo, x_hi], 1), jnp.concatenate([g_hi, g_hi, g_lo], 1)
        )
        dwr_ref[rows, STATE:] += mm_nt(
            jnp.concatenate([d_hi, d_lo, d_hi], 1), jnp.concatenate([s_hi, s_hi, s_lo], 1)
        )
        r_t = rt_ref[:, rows]
        grad = jnp.exp(end) * grad + mm(jnp.concatenate([r_t, r_t], 1), jnp.concatenate([d_hi, d_lo], 0))


def finish_kernel(*refs):
    *vp_refs, delta_ref, rate_ref, bias_ref, gd_ref, prm_ref = refs
    heads = delta_ref.shape[1]
    rate = jnp.exp(rate_ref[...])
    upper = jnp.where(iota((CHUNK, CHUNK), 1) >= iota((CHUNK, CHUNK), 0), 1.0, 0.0).astype(BF16)
    rate_sum = jnp.zeros((1, heads), F32)
    bias_sum = jnp.zeros((1, heads), F32)
    for c in range(delta_ref.shape[0] // CHUNK):
        rows = chunk_rows(c)
        vp = sum(ref[rows] for ref in vp_refs)
        hi, mid, lo = split3(vp)
        later = (mm(upper, hi) + mm(upper, mid) + mm(upper, lo))[:, :heads]
        pulled = vp[:, 2 * heads : 3 * heads]
        z = delta_ref[rows] + bias_ref[...]
        step = softplus(z)
        gate = 1.0 / (1.0 + jnp.exp(-z))
        ratio = jnp.where(step < 1e-30, 1.0, gate / jnp.maximum(step, 1e-30))
        grad = pulled * ratio - rate * later * gate
        gd_ref[rows] = grad
        rate_sum = rate_sum - rate * jnp.sum(later * step, axis=0, keepdims=True)
        bias_sum = bias_sum + jnp.sum(grad, axis=0, keepdims=True)
    prm_ref[0:1] = rate_sum
    prm_ref[1:2] = bias_sum


def params(limit_mib=40):
    return pltpu.CompilerParams(dimension_semantics=("arbitrary",), vmem_limit_bytes=limit_mib << 20)


def whole(*shape):
    return pl.BlockSpec(shape, lambda *ids: (0,) * len(shape))


def shards(
    mixer_input, write_vectors, read_vectors, delta_raw, log_rates, delta_bias, skip_gain, output_grad
):
    length, width = mixer_input.shape[1:]
    heads = delta_raw.shape[2]
    groups = write_vectors.shape[2] // STATE
    pairs = width // LANES
    per_group = pairs // groups
    group_width = width // groups
    depth = 6 * heads
    sds = jax.ShapeDtypeStruct
    x, dy = mixer_input[0], output_grad[0]
    w, r, delta = write_vectors[0], read_vectors[0], delta_raw[0]

    col = pl.BlockSpec((length, LANES), lambda j: (0, j))
    grp = pl.BlockSpec((length, STATE), lambda j: (0, j // per_group))
    grp_t = pl.BlockSpec((STATE, length), lambda j: (j // per_group, 0))
    pay_rows = 2 * STATE + TAIL
    pay, cs, ct, wt, rt = pl.pallas_call(
        functools.partial(prep_kernel, per_group=per_group),
        grid=(pairs,),
        in_specs=[col, col, grp, grp, whole(length, heads), whole(1, heads), whole(1, heads)],
        out_specs=[
            pl.BlockSpec((1, pay_rows, LANES), lambda j: (j, 0, 0)),
            whole(length, depth),
            whole(length // CHUNK, 2 * heads, CHUNK),
            grp_t,
            grp_t,
        ],
        out_shape=[
            sds((pairs, pay_rows, LANES), BF16),
            sds((length, depth), BF16),
            sds((length // CHUNK, 2 * heads, CHUNK), F32),
            sds((groups * STATE, length), BF16),
            sds((groups * STATE, length), BF16),
        ],
        compiler_params=params(),
        name="prep",
    )(x, dy, w, r, delta, log_rates, delta_bias)

    arrived = lax.all_to_all(pay, "ctx", split_axis=0, concat_axis=0, tiled=True)
    scanned = pl.pallas_call(
        scan_kernel,
        in_specs=[whole(pairs, pay_rows, LANES)],
        out_specs=whole(pairs, 2 * STATE, LANES),
        out_shape=sds((pairs, 2 * STATE, LANES), BF16),
        compiler_params=pltpu.CompilerParams(vmem_limit_bytes=40 << 20),
        grid=(1,),
        name="scan",
    )(arrived)
    edges = lax.all_to_all(scanned, "ctx", split_axis=0, concat_axis=0, tiled=True)

    skip_row = jnp.repeat(skip_gain, HEADDIM, axis=1)
    ups, vps, rows_out, skips = [], [], [], []
    for g in range(groups):
        first = g * per_group
        col_g = pl.BlockSpec((length, LANES), lambda p, first=first: (0, first + p))
        grp_g = pl.BlockSpec((length, STATE), lambda p, g=g: (0, g))
        out_col = pl.BlockSpec((length, LANES), lambda p: (0, p))
        dxi, vp, dwr, gsk = pl.pallas_call(
            functools.partial(intra_kernel, first_pair=first, heads=heads),
            grid=(per_group,),
            in_specs=[
                col_g, col_g, grp_g, grp_g, whole(length, depth), whole(length // CHUNK, 2 * heads, CHUNK),
                pl.BlockSpec((1, LANES), lambda p, first=first: (0, first + p)),
            ],
            out_specs=[out_col, whole(length, LANES), whole(length, 2 * STATE), whole(per_group, LANES)],
            out_shape=[
                sds((length, group_width), F32),
                sds((length, LANES), F32),
                sds((length, 2 * STATE), F32),
                sds((per_group, LANES), F32),
            ],
            scratch_shapes=[pltpu.VMEM((length // CHUNK, CHUNK, CHUNK), F32)] * 3,
            compiler_params=params(),
            name="intra",
        )(x, dy, w, r, cs, ct, skip_row)
        skips.append(gsk.reshape(per_group, 2, HEADDIM).sum(-1).reshape(1, -1))
        grp_tg = pl.BlockSpec((STATE, length), lambda p, g=g: (g, 0))
        up, vp, dwr = pl.pallas_call(
            functools.partial(inter_kernel, first_pair=first, heads=heads),
            grid=(per_group,),
            in_specs=[
                col_g, col_g, grp_g, grp_g, grp_tg, grp_tg, whole(length, depth),
                pl.BlockSpec((1, 2 * STATE, LANES), lambda p, first=first: (first + p, 0, 0)),
                out_col, whole(length, LANES), whole(length, 2 * STATE),
            ],
            out_specs=[out_col, whole(length, LANES), whole(length, 2 * STATE)],
            out_shape=[
                sds((length, group_width), BF16),
                sds((length, LANES), F32),
                sds((length, 2 * STATE), F32),
            ],
            scratch_shapes=[pltpu.VMEM((length // CHUNK + 1, STATE, LANES), F32)],
            compiler_params=params(),
            name="inter",
        )(x, dy, w, r, wt, rt, cs, edges, dxi, vp, dwr)
        ups.append(up)
        vps.append(vp)
        rows_out.append(dwr)

    grad_delta, sums = pl.pallas_call(
        finish_kernel,
        grid=(1,),
        in_specs=[whole(length, LANES)] * groups + [whole(length, heads), whole(1, heads), whole(1, heads)],
        out_specs=[whole(length, heads), whole(2, heads)],
        out_shape=[sds((length, heads), F32), sds((2, heads), F32)],
        compiler_params=params(),
        name="finish",
    )(*vps, delta, log_rates, delta_bias)

    devices = range(lax.axis_size("section"))
    route = [(i + 1, i) for i in devices if i + 1 in devices]
    upstream = jnp.concatenate([lax.ppermute(up, "section", route) for up in ups], axis=1)
    paired = jnp.concatenate(rows_out, axis=1)
    vector_rows = lax.all_to_all(paired, "tp", split_axis=0, concat_axis=1, tiled=True)
    mine = jnp.concatenate([sums, jnp.concatenate(skips, axis=1)], axis=0)
    places = lax.axis_size("ctx")
    spread = jnp.broadcast_to(mine[None], (places, *mine.shape))
    everyone = lax.all_to_all(spread, "ctx", split_axis=0, concat_axis=0, tiled=True)
    param_sums = jnp.sum(everyone, axis=0)
    return upstream[None], grad_delta[None], vector_rows[None], param_sums[None]


def solution(mesh):
    in_specs = (
        P("section", "ctx", "tp"),
        P("section", "ctx", "tp"),
        P("section", "ctx", "tp"),
        P("section", "ctx", "tp"),
        P("section", "tp"),
        P("section", "tp"),
        P("section", "tp"),
        P("section", "ctx", "tp"),
    )
    out_specs = (
        P("section", "ctx", "tp"),
        P("section", "ctx", "tp"),
        P("section", ("ctx", "tp"), None),
        P("section", None, "tp"),
    )
    return jax.shard_map(shards, mesh=mesh, in_specs=in_specs, out_specs=out_specs, check_vma=False)
```

```python
import functools

import jax
import jax.numpy as jnp
from jax import lax
from jax.experimental import pallas as pl
from jax.experimental.pallas import tpu as pltpu
from jax.sharding import PartitionSpec as P


HEADDIM = 64
STATE = 128
CHUNK = 128
LANES = 128
F32 = jnp.float32
BF16 = jnp.bfloat16
TAIL = 8


def iota(shape, dim):
    return lax.broadcasted_iota(jnp.int32, shape, dim)


def mm(a, b):
    return lax.dot_general(a, b, (((1,), (0,)), ((), ())), preferred_element_type=F32)


def mm_nt(a, b):
    return lax.dot_general(a, b, (((1,), (1,)), ((), ())), preferred_element_type=F32)


def split2(v):
    hi = v.astype(BF16)
    return hi, (v - hi.astype(F32)).astype(BF16)


def split3(v):
    hi = v.astype(BF16)
    rest = v - hi.astype(F32)
    mid = rest.astype(BF16)
    return hi, mid, (rest - mid.astype(F32)).astype(BF16)


def softplus(z):
    u = jnp.exp(-jnp.abs(z))
    small = u * (1.0 - u * (0.5 - u * (1.0 / 3.0 - u * (0.25 - u * 0.2))))
    return jnp.maximum(z, 0.0) + jnp.where(u < 0.03, small, jnp.log(1.0 + u))


def chunk_rows(c):
    return slice(c * CHUNK, (c + 1) * CHUNK)


def fill_expand_base(base_ref, heads):
    row, col = iota(base_ref.shape, 0), iota(base_ref.shape, 1)
    width = base_ref.shape[1] // 2
    kind = (row & (2 * heads - 1)) >= heads
    place = (col & (width - 1)) // HEADDIM
    base_ref[...] = jnp.where(kind == (col >= width), (row & (heads - 1)) - place, -64)


def expand(split, base_ref, first_head):
    hit = jnp.where(base_ref[...] == first_head, 1.0, 0.0).astype(BF16)
    out = mm(split, hit)
    width = out.shape[1] // 2
    return out[:, :width], out[:, width:]


def fill_sum_base(base_ref):
    row, col = iota(base_ref.shape, 0), iota(base_ref.shape, 1)
    base_ref[...] = col - (row & (LANES - 1)) // HEADDIM


def sum_pick(base_ref, column):
    return jnp.where(base_ref[...] == column, 1.0, 0.0).astype(BF16)


def head_sum(product, pick):
    return mm(jnp.concatenate(split2(product), axis=1), pick)


def row_ends(cl, chunks):
    return [cl[(c + 1) * CHUNK - 1 : (c + 1) * CHUNK] for c in range(chunks)]


def running(ends):
    before = [jnp.zeros_like(ends[0])]
    for end in ends:
        before.append(before[-1] + end)
    return before


def as_columns(row_ref, width):
    return jnp.concatenate([jnp.broadcast_to(row_ref[...], (LANES, row_ref.shape[1])).T] * (width // LANES), 1)


def prep_kernel(
    x_ref, dy_ref, w_ref, r_ref, delta_ref, rate_ref, bias_ref,
    pay_ref, low_ref, cs_ref, ct_ref, wt_ref, rt_ref, base_ref, *, steps_per_group
):
    quad = pl.program_id(0)
    length = x_ref.shape[0]
    heads = delta_ref.shape[0]
    chunks = length // CHUNK

    @pl.when(quad == 0)
    def _():
        fill_expand_base(base_ref, heads)
        step = softplus(delta_ref[...] + as_columns(bias_ref, length))
        logs = jnp.maximum(jnp.log(step), -200.0)
        decay = -step * jnp.exp(as_columns(rate_ref, length))
        upto = jnp.where(iota((CHUNK, CHUNK), 0) <= iota((CHUNK, CHUNK), 1), 1.0, 0.0).astype(BF16)
        for c in range(chunks):
            hi, mid, lo = split3(decay[:, chunk_rows(c)])
            cum = mm(hi, upto) + mm(mid, upto) + mm(lo, upto)
            both = jnp.concatenate([cum, cum - logs[:, chunk_rows(c)]], axis=0)
            ct_ref[c] = both
            cs_ref[chunk_rows(c), :] = jnp.concatenate(split3(both.T), axis=1)

    @pl.when(quad % steps_per_group == 0)
    def _():
        wt_ref[...] = w_ref[...].astype(F32).T.astype(BF16)
        rt_ref[...] = r_ref[...].astype(F32).T.astype(BF16)

    cl, ll = expand(cs_ref[...], base_ref, quad * (2 * LANES // HEADDIM))
    before = running(row_ends(cl, chunks))
    total = before[chunks]
    state = jnp.zeros((STATE, 2 * LANES), F32)
    grad = jnp.zeros((STATE, 2 * LANES), F32)
    for c in range(chunks):
        rows = chunk_rows(c)
        drawn = x_ref[rows].astype(F32) * jnp.exp((total - before[c]) - ll[rows])
        w_t, r_t = wt_ref[:, rows], rt_ref[:, rows]
        state += mm(jnp.concatenate([w_t, w_t], 1), jnp.concatenate(split2(drawn), 0))
        pushed = dy_ref[rows].astype(F32) * jnp.exp(before[c] + cl[rows])
        grad += mm(jnp.concatenate([r_t, r_t], 1), jnp.concatenate(split2(pushed), 0))
    carry = jnp.exp(total)
    carry_hi = carry.astype(BF16).astype(F32)
    picked = jnp.where(iota((TAIL, 2 * LANES), 0) == 0, carry_hi, carry - carry_hi).astype(BF16)
    state_hi, state_lo = split2(state)
    grad = grad.astype(BF16)
    for k in range(2):
        lanes = slice(k * LANES, (k + 1) * LANES)
        pay_ref[k, :STATE] = state_hi[:, lanes]
        pay_ref[k, STATE : 2 * STATE] = grad[:, lanes]
        pay_ref[k, 2 * STATE :] = picked[:, lanes]
        low_ref[k] = state_lo[:, lanes]


def scan_kernel(in_ref, out_ref):
    places = in_ref.shape[0]

    def carry(c):
        tail = in_ref[c, 2 * STATE :].astype(F32)
        return tail[0:1] + tail[1:2]

    state = jnp.zeros((STATE, LANES), F32)
    for c in range(places):
        out_ref[c, :STATE] = state.astype(BF16)
        state = carry(c) * state + in_ref[c, :STATE].astype(F32)
    grad = jnp.zeros((STATE, LANES), F32)
    for c in reversed(range(places)):
        out_ref[c, STATE:] = grad.astype(BF16)
        grad = carry(c) * grad + in_ref[c, STATE : 2 * STATE].astype(F32)


def local_kernel(
    x_ref, dy_ref, w_ref, r_ref, wt_ref, rt_ref, cs_ref, ct_ref, skip_ref,
    dxi_ref, vp_ref, dwr_ref, gsk_ref, pushed_ref, drawn_ref, tail_ref,
    sc_ref, sct_ref, dsc_ref, states_ref, base_ref, sum_base_ref, *, first_pair, heads
):
    place = pl.program_id(0)
    pair = first_pair + place
    length = x_ref.shape[0]
    chunks = length // CHUNK

    @pl.when(place == 0)
    def _():
        for c in range(chunks):
            rows = chunk_rows(c)
            sc_ref[c] = mm_nt(r_ref[rows], w_ref[rows])
            sct_ref[c] = mm_nt(w_ref[rows], r_ref[rows])
        dsc_ref[...] = jnp.zeros_like(dsc_ref)
        vp_ref[...] = jnp.zeros_like(vp_ref)
        dwr_ref[...] = jnp.zeros_like(dwr_ref)
        gsk_ref[...] = jnp.zeros_like(gsk_ref)
        fill_expand_base(base_ref, heads)
        fill_sum_base(sum_base_ref)

    cl, ll = expand(cs_ref[...], base_ref, 2 * pair)
    pick_push = sum_pick(sum_base_ref, 2 * pair)
    pick_drawn = sum_pick(sum_base_ref, 2 * heads + 2 * pair)
    row, col = iota((CHUNK, CHUNK), 0), iota((CHUNK, CHUNK), 1)
    left = iota((CHUNK, LANES), 1) < HEADDIM
    left_b = jnp.where(left, 1.0, 0.0).astype(BF16)
    right_b = jnp.where(left, 0.0, 1.0).astype(BF16)
    skip_sum = jnp.zeros((1, LANES), F32)
    ends = row_ends(cl, chunks)
    before = running(ends)

    state = None
    for c in range(chunks - 1):
        rows = chunk_rows(c)
        hi, lo = split2(x_ref[rows].astype(F32) * jnp.exp(ends[c] - ll[rows]))
        w_t = wt_ref[:, rows]
        written = mm(jnp.concatenate([w_t, w_t], 1), jnp.concatenate([hi, lo], 0))
        state = written if state is None else jnp.exp(ends[c]) * state + written
        states_ref[c + 1] = state

    grad = None
    for c in reversed(range(chunks)):
        rows = chunk_rows(c)
        x, dy = x_ref[rows], dy_ref[rows]
        xf, dyf = x.astype(F32), dy.astype(F32)
        x_two = jnp.concatenate([x * left_b, x * right_b], axis=0)
        dy_two = jnp.concatenate([dy * left_b, dy * right_b], axis=0)
        gram = mm_nt(dy, x_two)
        mixes, mixes_t = [], []
        total = dsc_ref[c]
        for k in range(2):
            lane = slice(k * HEADDIM, k * HEADDIM + 1)
            log_row = ct_ref[c, pl.ds(heads + 2 * pair + k, 1), :]
            decay = jnp.exp(jnp.where(row >= col, cl[rows, lane] - log_row, -1e30))
            mixes.append((sc_ref[c] * decay).astype(BF16))
            total = total + gram[:, k * CHUNK : (k + 1) * CHUNK] * decay
            cum_row = ct_ref[c, pl.ds(2 * pair + k, 1), :]
            decay_t = jnp.exp(jnp.where(col >= row, cum_row - ll[rows, lane], -1e30))
            mixes_t.append((sct_ref[c] * decay_t).astype(BF16))
        dsc_ref[c] = total
        y = mm(jnp.concatenate(mixes, axis=1), x_two)
        dx = mm(jnp.concatenate(mixes_t, axis=1), dy_two)
        seen = jnp.exp(cl[rows])
        pulled_y = dyf * seen
        if c > 0:
            r = r_ref[rows]
            s_hi, s_lo = split2(states_ref[c])
            y = y + seen * mm(jnp.concatenate([r, r], 1), jnp.concatenate([s_hi, s_lo], 0))
            d_hi, d_lo = split2(pulled_y)
            dwr_ref[rows, STATE:] += mm_nt(d_hi, s_hi)
        if grad is not None:
            w = w_ref[rows]
            tail = jnp.exp(ends[c] - ll[rows])
            g_hi, g_lo = split2(grad)
            dx = dx + tail * mm(jnp.concatenate([w, w], 1), jnp.concatenate([g_hi, g_lo], 0))
            dwr_ref[rows, :STATE] += mm_nt((xf * tail).astype(BF16), g_hi)
        if c > 0:
            r_t = rt_ref[:, rows]
            pulled = mm(jnp.concatenate([r_t, r_t], 1), jnp.concatenate([d_hi, d_lo], 0))
            grad = pulled if grad is None else jnp.exp(ends[c]) * grad + pulled
        drawn = xf * dx
        vp_ref[rows] += head_sum(dyf * y - drawn, pick_push) + head_sum(drawn, pick_drawn)
        dxi_ref[0, rows] = dx + skip_ref[...] * dyf
        skip_sum = skip_sum + jnp.sum(xf * dyf, axis=0, keepdims=True)
        pushed_ref[0, rows] = jnp.concatenate(split2(dyf * jnp.exp(before[c] + cl[rows])), 1)
        tail = jnp.exp((before[chunks] - before[c]) - ll[rows])
        drawn_ref[0, rows] = jnp.concatenate(split2(xf * tail), 1)
        tail_ref[0, rows] = tail
    gsk_ref[...] += head_sum(jnp.broadcast_to(skip_sum, (gsk_ref.shape[0], LANES)), pick_push)

    @pl.when(place == pl.num_programs(0) - 1)
    def _():
        for c in range(chunks):
            rows = chunk_rows(c)
            w, r = w_ref[rows], r_ref[rows]
            total = dsc_ref[c]
            hi, lo = split2(total)
            dwr_ref[rows, STATE:] += mm(jnp.concatenate([hi, lo], 1), jnp.concatenate([w, w], 0))
            hi, lo = split2(total.T)
            dwr_ref[rows, :STATE] += mm(jnp.concatenate([hi, lo], 1), jnp.concatenate([r, r], 0))


def inter_kernel(
    pushed_ref, drawn_ref, tail_ref, w_ref, r_ref, pay_ref, low_ref, st_ref, dxi_ref, vp_in_ref,
    gsk_ref, delta_ref, rate_ref, bias_ref, *refs, first_pair, heads, copies
):
    *refs, up_ref, gd_ref, prm_ref, vp_ref, sum_base_ref = refs
    place = pl.program_id(0)
    batch, length = pushed_ref.shape[:2]

    @pl.when(place == 0)
    def _():
        vp_ref[...] = vp_in_ref[...]
        fill_sum_base(sum_base_ref)

    sums = None
    for k in range(batch):
        pair = first_pair + place * batch + k
        state, grad = st_ref[k, :STATE], st_ref[k, STATE:]
        mark = pay_ref[k, 2 * STATE :].astype(F32)
        own = pay_ref[k, :STATE].astype(F32) + low_ref[k].astype(F32)
        ending = own + (mark[0:1] + mark[1:2]) * state.astype(F32)
        edge = jnp.sum(ending * grad.astype(F32), axis=0, keepdims=True)
        pushed, drawn = pushed_ref[k], drawn_ref[k]
        y = mm(r_ref[...], state)
        dx = mm(w_ref[...], grad)
        pulled = (drawn[:, :LANES].astype(F32) + drawn[:, LANES:].astype(F32)) * dx
        push = (pushed[:, :LANES].astype(F32) + pushed[:, LANES:].astype(F32)) * y - pulled
        push = push + jnp.where(iota((length, LANES), 0) == length - 1, edge, 0.0)
        found = head_sum(push, sum_pick(sum_base_ref, 2 * pair))
        found = found + head_sum(pulled, sum_pick(sum_base_ref, 2 * heads + 2 * pair))
        sums = found if sums is None else sums + found
        up_ref[:, k * LANES : (k + 1) * LANES] = (dxi_ref[k] + tail_ref[k] * dx).astype(BF16)
    vp_ref[...] += sums

    @pl.when(place == pl.num_programs(0) - 1)
    def _():
        rate = jnp.exp(as_columns(rate_ref, CHUNK))
        bias = as_columns(bias_ref, CHUNK)
        after = jnp.where(iota((CHUNK, CHUNK), 0) >= iota((CHUNK, CHUNK), 1), 1.0, 0.0).astype(BF16)
        rate_sum = jnp.zeros((heads, CHUNK), F32)
        bias_sum = jnp.zeros((heads, CHUNK), F32)
        beyond = jnp.zeros((heads, 1), F32)
        for c in reversed(range(length // CHUNK)):
            rows = chunk_rows(c)
            vp = vp_ref[rows].T
            hi, mid, lo = split3(vp[:heads])
            later = mm(hi, after) + mm(mid, after) + mm(lo, after) + beyond
            beyond = later[:, 0:1]
            z = delta_ref[:, rows] + bias
            step = softplus(z)
            gate = 1.0 / (1.0 + jnp.exp(-z))
            ratio = jnp.where(step < 1e-30, 1.0, gate / jnp.maximum(step, 1e-30))
            grad_delta = vp[2 * heads : 3 * heads] * ratio - rate * later * gate
            rate_sum = rate_sum - rate * later * step
            bias_sum = bias_sum + grad_delta
            if first_pair:
                grad_delta = grad_delta + refs[0][:, rows]
            gd_ref[:, rows] = grad_delta
        lane = iota((heads, LANES), 1)
        rate_sum = jnp.sum(rate_sum, axis=1, keepdims=True)
        bias_sum = jnp.sum(bias_sum, axis=1, keepdims=True)
        both = jnp.where(lane == 0, rate_sum, jnp.where(lane == 1, bias_sum, 0.0))
        both = jnp.concatenate([both, jnp.zeros((LANES - heads, LANES), F32)], 0).T[:8]
        sums = jnp.where(iota((8, LANES), 0) == 2, gsk_ref[...], both)
        if first_pair:
            sums = sums + refs[1][0]
        for k in range(copies):
            prm_ref[k] = sums


def vectors_kernel(me_ref, *refs, groups, places):
    out_refs, sum_ref = refs[4 * groups : -1], refs[-1]
    place = pl.program_id(0)
    length = refs[0].shape[1]
    for g in range(groups):
        pushed_ref, drawn_ref, st_ref, dwr_ref = refs[4 * g : 4 * g + 4]
        cols = slice(g * 2 * STATE, (g + 1) * 2 * STATE)

        @pl.when(place == 0)
        def _():
            sum_ref[:, cols] = dwr_ref[...]

        batch = pushed_ref.shape[0]
        half = g * 2 * STATE + STATE
        for ref, cols, part in (
            (drawn_ref, slice(half - STATE, half), slice(STATE, 2 * STATE)),
            (pushed_ref, slice(half, half + STATE), slice(0, STATE)),
        ):
            left = jnp.concatenate([ref[k] for k in range(batch)], axis=1)
            right = jnp.concatenate([st_ref[k, part] for k in range(batch) for _ in range(2)], axis=1)
            sum_ref[:, cols] += mm_nt(left, right)

    @pl.when(place == pl.num_programs(0) - 1)
    def _():
        rows = length // places
        for hop in range(places):
            start = pl.multiple_of(lax.rem(me_ref[0] + hop, places) * rows, rows)
            out_refs[hop][...] = sum_ref[pl.ds(start, rows), :].astype(BF16)


def rows_kernel(me_ref, *refs):
    *in_refs, out_ref = refs
    places = len(in_refs)
    width = in_refs[0].shape[1]
    for hop, ref in enumerate(in_refs):
        source = lax.rem(me_ref[0] + (places - hop), places)
        out_ref[:, pl.ds(pl.multiple_of(source * width, width), width)] = ref[...].astype(F32)


def params():
    return pltpu.CompilerParams(dimension_semantics=("arbitrary",), vmem_limit_bytes=67043328)


def cost(flops, moved):
    return pl.CostEstimate(flops=flops, bytes_accessed=moved, transcendentals=0)


def whole(*shape):
    return pl.BlockSpec(shape, lambda *ids: (0,) * len(shape))


def shards(
    mixer_input, write_vectors, read_vectors, delta_raw, log_rates, delta_bias, skip_gain, output_grad
):
    length, width = mixer_input.shape[1:]
    heads = delta_raw.shape[2]
    groups = write_vectors.shape[2] // STATE
    pairs = width // LANES
    per_group = pairs // groups
    group_width = width // groups
    depth = 6 * heads
    sds = jax.ShapeDtypeStruct
    x, dy = mixer_input[0], output_grad[0]
    w, r, delta = write_vectors[0], read_vectors[0], delta_raw[0].T

    steps = pairs // 2
    steps_per_group = steps // groups
    col = pl.BlockSpec((length, 2 * LANES), lambda j: (0, j))
    grp = pl.BlockSpec((length, STATE), lambda j: (0, j // steps_per_group))
    grp_t = pl.BlockSpec((STATE, length), lambda j: (j // steps_per_group, 0))
    pay_rows = 2 * STATE + TAIL
    pay, low, cs, ct, wt, rt = pl.pallas_call(
        functools.partial(prep_kernel, steps_per_group=steps_per_group),
        grid=(steps,),
        in_specs=[col, col, grp, grp, whole(heads, length), whole(1, heads), whole(1, heads)],
        out_specs=[
            pl.BlockSpec((2, pay_rows, LANES), lambda j: (j, 0, 0)),
            pl.BlockSpec((2, STATE, LANES), lambda j: (j, 0, 0)),
            whole(length, depth),
            whole(length // CHUNK, 2 * heads, CHUNK),
            grp_t,
            grp_t,
        ],
        out_shape=[
            sds((pairs, pay_rows, LANES), BF16),
            sds((pairs, STATE, LANES), BF16),
            sds((length, depth), BF16),
            sds((length // CHUNK, 2 * heads, CHUNK), F32),
            sds((groups * STATE, length), BF16),
            sds((groups * STATE, length), BF16),
        ],
        scratch_shapes=[pltpu.VMEM((depth, 4 * LANES), jnp.int32)],
        compiler_params=params(),
        name="prep",
    )(x, dy, w, r, delta, log_rates, delta_bias)

    skip_row = jnp.repeat(skip_gain, HEADDIM, axis=1)
    own_col = pl.BlockSpec((1, length, LANES), lambda p: (p, 0, 0))
    own_two = pl.BlockSpec((1, length, 2 * LANES), lambda p: (p, 0, 0))
    batch = 2
    trips = per_group // batch

    def many(*shape):
        return pl.BlockSpec((batch, *shape), lambda p: (p, 0, 0))

    def many_of(g, *shape):
        return pl.BlockSpec((batch, *shape), lambda p: (g * trips + p, 0, 0))

    me = lax.axis_index("tp")[None]
    places, copies = lax.axis_size("tp"), lax.axis_size("ctx")

    def group_specs(g):
        first = g * per_group
        col_g = pl.BlockSpec((length, LANES), lambda p: (0, first + p))
        grp_g = pl.BlockSpec((length, STATE), lambda p: (0, g))
        grp_tg = pl.BlockSpec((STATE, length), lambda p: (g, 0))
        return first, col_g, grp_g, grp_tg

    def local(g, cs):
        first, col_g, grp_g, grp_tg = group_specs(g)
        return pl.pallas_call(
            functools.partial(local_kernel, first_pair=first, heads=heads),
            grid=(per_group,),
            in_specs=[
                col_g, col_g, grp_g, grp_g, grp_tg, grp_tg, whole(length, depth),
                whole(length // CHUNK, 2 * heads, CHUNK),
                pl.BlockSpec((1, LANES), lambda p: (0, first + p)),
            ],
            out_specs=[
                own_col, whole(length, LANES), whole(length, 2 * STATE), whole(8, LANES), own_two, own_two, own_col
            ],
            out_shape=[
                sds((per_group, length, LANES), F32),
                sds((length, LANES), F32),
                sds((length, 2 * STATE), F32),
                sds((8, LANES), F32),
                sds((per_group, length, 2 * LANES), BF16),
                sds((per_group, length, 2 * LANES), BF16),
                sds((per_group, length, LANES), F32),
            ],
            scratch_shapes=[pltpu.VMEM((length // CHUNK, CHUNK, CHUNK), F32)] * 4
            + [pltpu.VMEM((depth, 2 * LANES), jnp.int32), pltpu.VMEM((2 * LANES, LANES), jnp.int32)],
            compiler_params=params(),
            cost_estimate=cost(20 * 10**9, 64 << 20),
            name="local",
        )(x, dy, w, r, wt, rt, cs, ct, skip_row)

    def inter(g, edges, own, carried):
        first, _, grp_g, _ = group_specs(g)
        dxi, vp, _, gsk, pushed, drawn, tail = own
        mine = copies if g == groups - 1 else 1
        return pl.pallas_call(
            functools.partial(inter_kernel, first_pair=first, heads=heads, copies=mine),
            grid=(trips,),
            in_specs=[
                many(length, 2 * LANES), many(length, 2 * LANES), many(length, LANES), grp_g, grp_g,
                many_of(g, pay_rows, LANES), many_of(g, STATE, LANES), many_of(g, 2 * STATE, LANES),
                many(length, LANES), whole(length, LANES), whole(8, LANES),
                whole(heads, length), whole(1, heads), whole(1, heads), *[whole(*a.shape) for a in carried],
            ],
            out_specs=[
                pl.BlockSpec((length, batch * LANES), lambda p: (0, p)), whole(heads, length), whole(mine, 8, LANES)
            ],
            out_shape=[sds((length, group_width), BF16), sds((heads, length), F32), sds((mine, 8, LANES), F32)],
            scratch_shapes=[pltpu.VMEM((length, LANES), F32), pltpu.VMEM((2 * LANES, LANES), jnp.int32)],
            compiler_params=params(),
            cost_estimate=cost(4 * 10**9, 16 << 20),
            name="inter",
        )(pushed, drawn, tail, w, r, pay, low, edges, dxi, vp, gsk, delta, log_rates, delta_bias, *carried)

    arrived = lax.all_to_all(pay, "ctx", split_axis=0, concat_axis=0, tiled=True)
    own = [local(0, cs)]
    arrived, own[0] = lax.optimization_barrier((arrived, own[0]))
    scanned = pl.pallas_call(
        scan_kernel,
        in_specs=[whole(pairs, pay_rows, LANES)],
        out_specs=whole(pairs, 2 * STATE, LANES),
        out_shape=sds((pairs, 2 * STATE, LANES), BF16),
        compiler_params=params(),
        grid=(1,),
        name="scan",
    )(arrived)
    scanned, cs_later = lax.optimization_barrier((scanned, cs))
    edges = lax.all_to_all(scanned, "ctx", split_axis=0, concat_axis=0, tiled=True)
    own += [local(g, cs_later) for g in range(1, groups)]
    edges, own = lax.optimization_barrier((edges, own))

    devices = range(lax.axis_size("section"))
    route = [(i + 1, i) for i in devices if i + 1 in devices]
    ups, carried = [], []
    for g in range(groups):
        up, *carried = inter(g, edges, own[g], carried)
        ups.append(lax.ppermute(up, "section", route))
    grad_delta, sums = carried
    everyone = lax.all_to_all(sums, "ctx", split_axis=0, concat_axis=0, tiled=True)

    param_sums = jnp.sum(everyone, axis=0)[:3, :heads]
    upstream = jnp.concatenate(ups, axis=1)
    row_shape = (length // places, groups * 2 * STATE)
    pieces = [a for g in range(groups) for a in (own[g][4], own[g][5], edges, own[g][2])]
    row_blocks = pl.pallas_call(
        functools.partial(vectors_kernel, groups=groups, places=places),
        grid=(trips,),
        in_specs=[pl.BlockSpec(memory_space=pltpu.SMEM)]
        + [
            spec
            for g in range(groups)
            for spec in (
                many(length, 2 * LANES), many(length, 2 * LANES), many_of(g, 2 * STATE, LANES), whole(length, 2 * STATE)
            )
        ],
        out_specs=[whole(*row_shape)] * places,
        out_shape=[sds(row_shape, BF16)] * places,
        scratch_shapes=[pltpu.VMEM((length, row_shape[1]), F32)],
        compiler_params=params(),
        cost_estimate=cost(4 * 10**9, 16 << 20),
        name="vectors",
    )(me, *pieces)
    got = [
        lax.ppermute(part, "tp", [(i, (i + hop) % places) for i in range(places)]) if hop else part
        for hop, part in enumerate(row_blocks)
    ]
    upstream, param_sums, got = lax.optimization_barrier((upstream, param_sums, got))
    vector_rows = pl.pallas_call(
        rows_kernel,
        grid=(1,),
        in_specs=[pl.BlockSpec(memory_space=pltpu.SMEM)] + [whole(*row_shape)] * places,
        out_specs=whole(row_shape[0], row_shape[1] * places),
        out_shape=sds((row_shape[0], row_shape[1] * places), F32),
        compiler_params=params(),
        name="rows",
    )(me, *got)
    return upstream[None], grad_delta.T[None], vector_rows[None], param_sums[None]


def solution(mesh):
    in_specs = (
        P("section", "ctx", "tp"),
        P("section", "ctx", "tp"),
        P("section", "ctx", "tp"),
        P("section", "ctx", "tp"),
        P("section", "tp"),
        P("section", "tp"),
        P("section", "tp"),
        P("section", "ctx", "tp"),
    )
    out_specs = (
        P("section", "ctx", "tp"),
        P("section", "ctx", "tp"),
        P("section", ("ctx", "tp"), None),
        P("section", None, "tp"),
    )

    return jax.shard_map(shards, mesh=mesh, in_specs=in_specs, out_specs=out_specs, check_vma=False)
```

```python
import functools

import jax
import jax.numpy as jnp
from jax import lax
from jax.experimental import pallas as pl
from jax.experimental.pallas import tpu as pltpu
from jax.sharding import PartitionSpec as P


HEADDIM = 64
STATE = 128
CHUNK = 128
LANES = 128
F32 = jnp.float32
BF16 = jnp.bfloat16
TAIL = 8


def iota(shape, dim):
    return lax.broadcasted_iota(jnp.int32, shape, dim)


def mm(a, b):
    return lax.dot_general(a, b, (((1,), (0,)), ((), ())), preferred_element_type=F32)


def mm_nt(a, b):
    return lax.dot_general(a, b, (((1,), (1,)), ((), ())), preferred_element_type=F32)


def split2(v):
    hi = v.astype(BF16)
    return hi, (v - hi.astype(F32)).astype(BF16)


def split3(v):
    hi = v.astype(BF16)
    rest = v - hi.astype(F32)
    mid = rest.astype(BF16)
    return hi, mid, (rest - mid.astype(F32)).astype(BF16)


def softplus(z):
    u = jnp.exp(-jnp.abs(z))
    small = u * (1.0 - u * (0.5 - u * (1.0 / 3.0 - u * (0.25 - u * 0.2))))
    return jnp.maximum(z, 0.0) + jnp.where(u < 0.03, small, jnp.log(1.0 + u))


def chunk_rows(c):
    return slice(c * CHUNK, (c + 1) * CHUNK)


def fill_expand_base(base_ref, heads):
    row, col = iota(base_ref.shape, 0), iota(base_ref.shape, 1)
    width = base_ref.shape[1] // 2
    kind = (row & (2 * heads - 1)) >= heads
    place = (col & (width - 1)) // HEADDIM
    base_ref[...] = jnp.where(kind == (col >= width), (row & (heads - 1)) - place, -64)


def expand(split, base_ref, first_head):
    hit = jnp.where(base_ref[...] == first_head, 1.0, 0.0).astype(BF16)
    out = mm(split, hit)
    width = out.shape[1] // 2
    return out[:, :width], out[:, width:]


def fill_sum_base(base_ref):
    row, col = iota(base_ref.shape, 0), iota(base_ref.shape, 1)
    base_ref[...] = col - (row & (LANES - 1)) // HEADDIM


def sum_pick(base_ref, column):
    return jnp.where(base_ref[...] == column, 1.0, 0.0).astype(BF16)


def head_sum(product, pick):
    return mm(jnp.concatenate(split2(product), axis=1), pick)


def row_ends(cl, chunks):
    return [cl[(c + 1) * CHUNK - 1 : (c + 1) * CHUNK] for c in range(chunks)]


def running(ends):
    before = [jnp.zeros_like(ends[0])]
    for end in ends:
        before.append(before[-1] + end)
    return before


def as_columns(row_ref, width):
    return jnp.concatenate([jnp.broadcast_to(row_ref[...], (LANES, row_ref.shape[1])).T] * (width // LANES), 1)


def prep_kernel(
    x_ref, dy_ref, w_ref, r_ref, delta_ref, rate_ref, bias_ref,
    pay_ref, low_ref, cs_ref, ct_ref, wt_ref, rt_ref, base_ref, *, steps_per_group
):
    quad = pl.program_id(0)
    length = x_ref.shape[0]
    heads = delta_ref.shape[0]
    chunks = length // CHUNK

    @pl.when(quad == 0)
    def _():
        fill_expand_base(base_ref, heads)
        step = softplus(delta_ref[...] + as_columns(bias_ref, length))
        logs = jnp.maximum(jnp.log(step), -200.0)
        decay = -step * jnp.exp(as_columns(rate_ref, length))
        upto = jnp.where(iota((CHUNK, CHUNK), 0) <= iota((CHUNK, CHUNK), 1), 1.0, 0.0).astype(BF16)
        for c in range(chunks):
            hi, mid, lo = split3(decay[:, chunk_rows(c)])
            cum = mm(hi, upto) + mm(mid, upto) + mm(lo, upto)
            both = jnp.concatenate([cum, cum - logs[:, chunk_rows(c)]], axis=0)
            ct_ref[c] = both
            cs_ref[chunk_rows(c), :] = jnp.concatenate(split3(both.T), axis=1)

    @pl.when(quad % steps_per_group == 0)
    def _():
        wt_ref[...] = w_ref[...].astype(F32).T.astype(BF16)
        rt_ref[...] = r_ref[...].astype(F32).T.astype(BF16)

    cl, ll = expand(cs_ref[...], base_ref, quad * (2 * LANES // HEADDIM))
    before = running(row_ends(cl, chunks))
    total = before[chunks]
    state = jnp.zeros((STATE, 2 * LANES), F32)
    grad = jnp.zeros((STATE, 2 * LANES), F32)
    for c in range(chunks):
        rows = chunk_rows(c)
        drawn = x_ref[rows].astype(F32) * jnp.exp((total - before[c]) - ll[rows])
        w_t, r_t = wt_ref[:, rows], rt_ref[:, rows]
        state += mm(jnp.concatenate([w_t, w_t], 1), jnp.concatenate(split2(drawn), 0))
        pushed = dy_ref[rows].astype(F32) * jnp.exp(before[c] + cl[rows])
        grad += mm(jnp.concatenate([r_t, r_t], 1), jnp.concatenate(split2(pushed), 0))
    carry = jnp.exp(total)
    carry_hi = carry.astype(BF16).astype(F32)
    picked = jnp.where(iota((TAIL, 2 * LANES), 0) == 0, carry_hi, carry - carry_hi).astype(BF16)
    state_hi, state_lo = split2(state)
    grad = grad.astype(BF16)
    for k in range(2):
        lanes = slice(k * LANES, (k + 1) * LANES)
        pay_ref[k, :STATE] = state_hi[:, lanes]
        pay_ref[k, STATE : 2 * STATE] = grad[:, lanes]
        pay_ref[k, 2 * STATE :] = picked[:, lanes]
        low_ref[k] = state_lo[:, lanes]


def scan_kernel(in_ref, mark_ref, out_ref):
    places = in_ref.shape[0]

    def run(order):
        total = jnp.zeros((STATE, LANES), F32)
        for c in order:
            out_ref[c] = total.astype(BF16)
            mark = mark_ref[c].astype(F32)
            total = (mark[0:1] + mark[1:2]) * total + in_ref[c].astype(F32)

    @pl.when(pl.program_id(0) == 0)
    def _():
        run(range(places))

    @pl.when(pl.program_id(0) == 1)
    def _():
        run(reversed(range(places)))


def local_kernel(
    x_ref, dy_ref, w_ref, r_ref, wt_ref, rt_ref, cs_ref, ct_ref, skip_ref,
    dxi_ref, vp_ref, dwr_ref, gsk_ref, pushed_ref, tail_ref,
    sc_ref, sct_ref, dsc_ref, states_ref, base_ref, sum_base_ref, *, first_pair, heads
):
    place = pl.program_id(0)
    pair = first_pair + place
    length = x_ref.shape[0]
    chunks = length // CHUNK

    @pl.when(place == 0)
    def _():
        for c in range(chunks):
            rows = chunk_rows(c)
            sc_ref[c] = mm_nt(r_ref[rows], w_ref[rows])
            sct_ref[c] = mm_nt(w_ref[rows], r_ref[rows])
        dsc_ref[...] = jnp.zeros_like(dsc_ref)
        vp_ref[...] = jnp.zeros_like(vp_ref)
        dwr_ref[...] = jnp.zeros_like(dwr_ref)
        gsk_ref[...] = jnp.zeros_like(gsk_ref)
        fill_expand_base(base_ref, heads)
        fill_sum_base(sum_base_ref)

    cl, ll = expand(cs_ref[...], base_ref, 2 * pair)
    pick_push = sum_pick(sum_base_ref, 2 * pair)
    pick_drawn = sum_pick(sum_base_ref, 2 * heads + 2 * pair)
    row, col = iota((CHUNK, CHUNK), 0), iota((CHUNK, CHUNK), 1)
    left = iota((CHUNK, LANES), 1) < HEADDIM
    left_b = jnp.where(left, 1.0, 0.0).astype(BF16)
    right_b = jnp.where(left, 0.0, 1.0).astype(BF16)
    skip_sum = jnp.zeros((1, LANES), F32)
    ends = row_ends(cl, chunks)
    before = running(ends)

    state = None
    for c in range(chunks - 1):
        rows = chunk_rows(c)
        hi, lo = split2(x_ref[rows].astype(F32) * jnp.exp(ends[c] - ll[rows]))
        w_t = wt_ref[:, rows]
        written = mm(jnp.concatenate([w_t, w_t], 1), jnp.concatenate([hi, lo], 0))
        state = written if state is None else jnp.exp(ends[c]) * state + written
        states_ref[c + 1] = state

    grad = None
    for c in reversed(range(chunks)):
        rows = chunk_rows(c)
        x, dy = x_ref[rows], dy_ref[rows]
        xf, dyf = x.astype(F32), dy.astype(F32)
        x_two = jnp.concatenate([x * left_b, x * right_b], axis=0)
        dy_two = jnp.concatenate([dy * left_b, dy * right_b], axis=0)
        gram = mm_nt(dy, x_two)
        mixes, mixes_t = [], []
        total = dsc_ref[c]
        for k in range(2):
            lane = slice(k * HEADDIM, k * HEADDIM + 1)
            log_row = ct_ref[c, pl.ds(heads + 2 * pair + k, 1), :]
            decay = jnp.exp(jnp.where(row >= col, cl[rows, lane] - log_row, -1e30))
            mixes.append((sc_ref[c] * decay).astype(BF16))
            total = total + gram[:, k * CHUNK : (k + 1) * CHUNK] * decay
            cum_row = ct_ref[c, pl.ds(2 * pair + k, 1), :]
            decay_t = jnp.exp(jnp.where(col >= row, cum_row - ll[rows, lane], -1e30))
            mixes_t.append((sct_ref[c] * decay_t).astype(BF16))
        dsc_ref[c] = total
        y = mm(jnp.concatenate(mixes, axis=1), x_two)
        dx = mm(jnp.concatenate(mixes_t, axis=1), dy_two)
        seen = jnp.exp(cl[rows])
        pulled_y = dyf * seen
        if c > 0:
            r = r_ref[rows]
            s_hi, s_lo = split2(states_ref[c])
            y = y + seen * mm(jnp.concatenate([r, r], 1), jnp.concatenate([s_hi, s_lo], 0))
            d_hi, d_lo = split2(pulled_y)
            dwr_ref[rows, STATE:] += mm_nt(d_hi, s_hi)
        if grad is not None:
            w = w_ref[rows]
            tail = jnp.exp(ends[c] - ll[rows])
            g_hi, g_lo = split2(grad)
            dx = dx + tail * mm(jnp.concatenate([w, w], 1), jnp.concatenate([g_hi, g_lo], 0))
            dwr_ref[rows, :STATE] += mm_nt((xf * tail).astype(BF16), g_hi)
        if c > 0:
            r_t = rt_ref[:, rows]
            pulled = mm(jnp.concatenate([r_t, r_t], 1), jnp.concatenate([d_hi, d_lo], 0))
            grad = pulled if grad is None else jnp.exp(ends[c]) * grad + pulled
        drawn = xf * dx
        vp_ref[rows] += head_sum(dyf * y - drawn, pick_push) + head_sum(drawn, pick_drawn)
        dxi_ref[0, rows] = dx + skip_ref[...] * dyf
        skip_sum = skip_sum + jnp.sum(xf * dyf, axis=0, keepdims=True)
        pushed_ref[0, rows] = jnp.concatenate(split2(dyf * jnp.exp(before[c] + cl[rows])), 1)
        tail = jnp.exp((before[chunks] - before[c]) - ll[rows])
        tail_ref[0, rows] = tail
    gsk_ref[...] += head_sum(jnp.broadcast_to(skip_sum, (gsk_ref.shape[0], LANES)), pick_push)

    @pl.when(place == pl.num_programs(0) - 1)
    def _():
        for c in range(chunks):
            rows = chunk_rows(c)
            w, r = w_ref[rows], r_ref[rows]
            total = dsc_ref[c]
            hi, lo = split2(total)
            dwr_ref[rows, STATE:] += mm(jnp.concatenate([hi, lo], 1), jnp.concatenate([w, w], 0))
            hi, lo = split2(total.T)
            dwr_ref[rows, :STATE] += mm(jnp.concatenate([hi, lo], 1), jnp.concatenate([r, r], 0))


def inter_kernel(
    me_ref, pushed_ref, tail_ref, x_ref, w_ref, r_ref, pay_ref, low_ref, st_ref, dxi_ref, vp_in_ref, dwr_in_ref,
    gsk_ref, delta_ref, rate_ref, bias_ref, *refs, first_pair, heads, copies, places
):
    *refs, vp_ref, sum_ref, sum_base_ref = refs
    if first_pair:
        gd_in_ref, prm_in_ref, rows_in_ref, *refs = refs
    up_ref, gd_ref, prm_ref, *rows_refs = refs
    place = pl.program_id(0)
    batch, length = pushed_ref.shape[:2]

    @pl.when(place == 0)
    def _():
        vp_ref[...] = vp_in_ref[...]
        sum_ref[...] = dwr_in_ref[...]
        fill_sum_base(sum_base_ref)

    sums = None
    drawn_parts, pushed_parts, grads, states = [], [], [], []
    for k in range(batch):
        pair = first_pair + place * batch + k
        lanes = slice(k * LANES, (k + 1) * LANES)
        state, grad = st_ref[k, :STATE], st_ref[k, STATE:]
        mark = pay_ref[k, 2 * STATE :].astype(F32)
        own = pay_ref[k, :STATE].astype(F32) + low_ref[k].astype(F32)
        ending = own + (mark[0:1] + mark[1:2]) * state.astype(F32)
        edge = jnp.sum(ending * grad.astype(F32), axis=0, keepdims=True)
        pushed, tail = pushed_ref[k], tail_ref[k]
        drawn = x_ref[:, lanes].astype(F32) * tail
        y = mm(r_ref[...], state)
        dx = mm(w_ref[...], grad)
        pulled = drawn * dx
        push = (pushed[:, :LANES].astype(F32) + pushed[:, LANES:].astype(F32)) * y - pulled
        push = push + jnp.where(iota((length, LANES), 0) == length - 1, edge, 0.0)
        found = head_sum(push, sum_pick(sum_base_ref, 2 * pair))
        found = found + head_sum(pulled, sum_pick(sum_base_ref, 2 * heads + 2 * pair))
        sums = found if sums is None else sums + found
        up_ref[:, lanes] = (dxi_ref[k] + tail * dx).astype(BF16)
        drawn_parts += split2(drawn)
        pushed_parts.append(pushed)
        grads += [grad, grad]
        states += [state, state]
    vp_ref[...] += sums
    sum_ref[:, :STATE] += mm_nt(jnp.concatenate(drawn_parts, 1), jnp.concatenate(grads, 1))
    sum_ref[:, STATE:] += mm_nt(jnp.concatenate(pushed_parts, 1), jnp.concatenate(states, 1))

    @pl.when(place == pl.num_programs(0) - 1)
    def _():
        rate = jnp.exp(as_columns(rate_ref, CHUNK))
        bias = as_columns(bias_ref, CHUNK)
        after = jnp.where(iota((CHUNK, CHUNK), 0) >= iota((CHUNK, CHUNK), 1), 1.0, 0.0).astype(BF16)
        rate_sum = jnp.zeros((heads, CHUNK), F32)
        bias_sum = jnp.zeros((heads, CHUNK), F32)
        beyond = jnp.zeros((heads, 1), F32)
        for c in reversed(range(length // CHUNK)):
            rows = chunk_rows(c)
            vp = vp_ref[rows].T
            hi, mid, lo = split3(vp[:heads])
            later = mm(hi, after) + mm(mid, after) + mm(lo, after) + beyond
            beyond = later[:, 0:1]
            z = delta_ref[:, rows] + bias
            step = softplus(z)
            gate = 1.0 / (1.0 + jnp.exp(-z))
            ratio = jnp.where(step < 1e-30, 1.0, gate / jnp.maximum(step, 1e-30))
            grad_delta = vp[2 * heads : 3 * heads] * ratio - rate * later * gate
            rate_sum = rate_sum - rate * later * step
            bias_sum = bias_sum + grad_delta
            if first_pair:
                grad_delta = grad_delta + gd_in_ref[:, rows]
            gd_ref[:, rows] = grad_delta
        lane = iota((heads, LANES), 1)
        rate_sum = jnp.sum(rate_sum, axis=1, keepdims=True)
        bias_sum = jnp.sum(bias_sum, axis=1, keepdims=True)
        both = jnp.where(lane == 0, rate_sum, jnp.where(lane == 1, bias_sum, 0.0))
        both = jnp.concatenate([both, jnp.zeros((LANES - heads, LANES), F32)], 0).T[:8]
        sums = jnp.where(iota((8, LANES), 0) == 2, gsk_ref[...], both)
        if first_pair:
            sums = sums + prm_in_ref[0]
        for k in range(copies):
            prm_ref[k] = sums
        rows = length // len(rows_refs)
        for hop, ref in enumerate(rows_refs):
            start = pl.multiple_of(lax.rem(me_ref[0] + hop, places) * rows, rows) if len(rows_refs) > 1 else 0
            if first_pair:
                ref[:, : -2 * STATE] = rows_in_ref[pl.ds(start, rows), :]
            ref[:, -2 * STATE :] = sum_ref[pl.ds(start, rows), :].astype(BF16)


def first_kernel(in_ref, out_ref):
    out_ref[...] = in_ref[...]


def last_kernel(me_ref, buffer_ref, up_ref, *refs):
    *in_refs, all_ref, out_ref = refs
    all_ref[...] = up_ref[...]
    places = len(in_refs)
    width = in_refs[0].shape[1]
    for hop, ref in enumerate(in_refs):
        source = lax.rem(me_ref[0] + (places - hop), places)
        out_ref[:, pl.ds(pl.multiple_of(source * width, width), width)] = ref[...].astype(F32)


def params():
    return pltpu.CompilerParams(dimension_semantics=("arbitrary",), vmem_limit_bytes=67043328)


def cost(flops, moved):
    return pl.CostEstimate(flops=flops, bytes_accessed=moved, transcendentals=0)


def whole(*shape):
    return pl.BlockSpec(shape, lambda *ids: (0,) * len(shape))


def shards(
    mixer_input, write_vectors, read_vectors, delta_raw, log_rates, delta_bias, skip_gain, output_grad
):
    length, width = mixer_input.shape[1:]
    heads = delta_raw.shape[2]
    groups = write_vectors.shape[2] // STATE
    pairs = width // LANES
    per_group = pairs // groups
    group_width = width // groups
    depth = 6 * heads
    sds = jax.ShapeDtypeStruct
    x, dy = mixer_input[0], output_grad[0]
    w, r, delta = write_vectors[0], read_vectors[0], delta_raw[0].T

    steps = pairs // 2
    steps_per_group = steps // groups
    col = pl.BlockSpec((length, 2 * LANES), lambda j: (0, j))
    grp = pl.BlockSpec((length, STATE), lambda j: (0, j // steps_per_group))
    grp_t = pl.BlockSpec((STATE, length), lambda j: (j // steps_per_group, 0))
    pay_rows = 2 * STATE + TAIL
    pay, low, cs, ct, wt, rt = pl.pallas_call(
        functools.partial(prep_kernel, steps_per_group=steps_per_group),
        grid=(steps,),
        in_specs=[col, col, grp, grp, whole(heads, length), whole(1, heads), whole(1, heads)],
        out_specs=[
            pl.BlockSpec((2, pay_rows, LANES), lambda j: (j, 0, 0)),
            pl.BlockSpec((2, STATE, LANES), lambda j: (j, 0, 0)),
            whole(length, depth),
            whole(length // CHUNK, 2 * heads, CHUNK),
            grp_t,
            grp_t,
        ],
        out_shape=[
            sds((pairs, pay_rows, LANES), BF16),
            sds((pairs, STATE, LANES), BF16),
            sds((length, depth), BF16),
            sds((length // CHUNK, 2 * heads, CHUNK), F32),
            sds((groups * STATE, length), BF16),
            sds((groups * STATE, length), BF16),
        ],
        scratch_shapes=[pltpu.VMEM((depth, 4 * LANES), jnp.int32)],
        compiler_params=params(),
        name="prep",
    )(x, dy, w, r, delta, log_rates, delta_bias)

    skip_row = jnp.repeat(skip_gain, HEADDIM, axis=1)
    own_col = pl.BlockSpec((1, length, LANES), lambda p: (p, 0, 0))
    own_two = pl.BlockSpec((1, length, 2 * LANES), lambda p: (p, 0, 0))
    batch = 2
    trips = per_group // batch

    def many(*shape):
        return pl.BlockSpec((batch, *shape), lambda p: (p, 0, 0))

    def many_of(g, *shape):
        return pl.BlockSpec((batch, *shape), lambda p: (g * trips + p, 0, 0))

    me = lax.axis_index("tp")[None]
    places, copies = lax.axis_size("tp"), lax.axis_size("ctx")

    def group_specs(g):
        first = g * per_group
        col_g = pl.BlockSpec((length, LANES), lambda p: (0, first + p))
        grp_g = pl.BlockSpec((length, STATE), lambda p: (0, g))
        grp_tg = pl.BlockSpec((STATE, length), lambda p: (g, 0))
        return first, col_g, grp_g, grp_tg

    def local(g, cs):
        first, col_g, grp_g, grp_tg = group_specs(g)
        return pl.pallas_call(
            functools.partial(local_kernel, first_pair=first, heads=heads),
            grid=(per_group,),
            in_specs=[
                col_g, col_g, grp_g, grp_g, grp_tg, grp_tg, whole(length, depth),
                whole(length // CHUNK, 2 * heads, CHUNK),
                pl.BlockSpec((1, LANES), lambda p: (0, first + p)),
            ],
            out_specs=[
                own_col, whole(length, LANES), whole(length, 2 * STATE), whole(8, LANES), own_two, own_col
            ],
            out_shape=[
                sds((per_group, length, LANES), F32),
                sds((length, LANES), F32),
                sds((length, 2 * STATE), F32),
                sds((8, LANES), F32),
                sds((per_group, length, 2 * LANES), BF16),
                sds((per_group, length, LANES), F32),
            ],
            scratch_shapes=[pltpu.VMEM((length // CHUNK, CHUNK, CHUNK), F32)] * 4
            + [pltpu.VMEM((depth, 2 * LANES), jnp.int32), pltpu.VMEM((2 * LANES, LANES), jnp.int32)],
            compiler_params=params(),
            cost_estimate=cost(20 * 10**9, 64 << 20),
            name="local",
        )(x, dy, w, r, wt, rt, cs, ct, skip_row)

    def inter(g, edges, own, carried):
        first, _, grp_g, _ = group_specs(g)
        dxi, vp, dwr, gsk, pushed, tail = own
        final = g == groups - 1
        mine = copies if final else 1
        row_width = 2 * STATE * (g + 1)
        row_shapes = [(length // places, row_width)] * places if final else [(length, row_width)]
        return pl.pallas_call(
            functools.partial(inter_kernel, first_pair=first, heads=heads, copies=mine, places=places),
            grid=(trips,),
            in_specs=[
                pl.BlockSpec(memory_space=pltpu.SMEM),
                many(length, 2 * LANES), many(length, LANES),
                pl.BlockSpec((length, batch * LANES), lambda p: (0, g * trips + p)), grp_g, grp_g,
                many_of(g, pay_rows, LANES), many_of(g, STATE, LANES), many_of(g, 2 * STATE, LANES),
                many(length, LANES), whole(length, LANES), whole(length, 2 * STATE), whole(8, LANES),
                whole(heads, length), whole(1, heads), whole(1, heads), *[whole(*a.shape) for a in carried],
            ],
            out_specs=[
                pl.BlockSpec((length, batch * LANES), lambda p: (0, p)), whole(heads, length), whole(mine, 8, LANES),
                *[whole(*shape) for shape in row_shapes],
            ],
            out_shape=[
                sds((length, group_width), BF16), sds((heads, length), F32), sds((mine, 8, LANES), F32),
                *[sds(shape, BF16) for shape in row_shapes],
            ],
            scratch_shapes=[
                pltpu.VMEM((length, LANES), F32),
                pltpu.VMEM((length, 2 * STATE), F32),
                pltpu.VMEM((2 * LANES, LANES), jnp.int32),
            ],
            compiler_params=params(),
            cost_estimate=cost(4 * 10**9, 16 << 20),
            name="inter",
        )(me, pushed, tail, x, w, r, pay, low, edges, dxi, vp, dwr, gsk, delta, log_rates, delta_bias, *carried)

    arrived = lax.all_to_all(pay, "ctx", split_axis=0, concat_axis=0, tiled=True)
    own = [local(0, cs)]
    arrived, own[0] = lax.optimization_barrier((arrived, own[0]))
    scanned = pl.pallas_call(
        scan_kernel,
        in_specs=[
            pl.BlockSpec((pairs, STATE, LANES), lambda i: (0, i, 0)),
            pl.BlockSpec((pairs, TAIL, LANES), lambda i: (0, 2 * STATE // TAIL, 0)),
        ],
        out_specs=pl.BlockSpec((pairs, STATE, LANES), lambda i: (0, i, 0)),
        out_shape=sds((pairs, 2 * STATE, LANES), BF16),
        compiler_params=params(),
        grid=(2,),
        name="scan",
    )(arrived, arrived)
    scanned, cs_later = lax.optimization_barrier((scanned, cs))
    edges = lax.all_to_all(scanned, "ctx", split_axis=0, concat_axis=0, tiled=True)
    own += [local(g, cs_later) for g in range(1, groups)]
    edges, own = lax.optimization_barrier((edges, own))

    devices = range(lax.axis_size("section"))
    route = [(i + 1, i) for i in devices if i + 1 in devices]
    ups, carried = [], []
    for g in range(groups):
        up, *carried = inter(g, edges, own[g], carried)
        ups.append(lax.ppermute(up, "section", route))
    grad_delta, sums, *row_blocks = carried
    everyone = lax.all_to_all(sums, "ctx", split_axis=0, concat_axis=0, tiled=True)
    got = row_blocks[:1]
    for hop in range(1, places):
        got.append(lax.ppermute(row_blocks[hop], "tp", [(i, (i + hop) % places) for i in range(places)]))
    param_sums = jnp.sum(everyone, axis=0)[:3, :heads]
    before = width - group_width
    start = jnp.concatenate(ups[:-1], axis=1) if groups > 2 else ups[0]
    buffer = pl.pallas_call(
        first_kernel,
        grid=(1,),
        in_specs=[whole(length, before)],
        out_specs=whole(length, before),
        out_shape=sds((length, width), BF16),
        compiler_params=params(),
        cost_estimate=cost(10**6, 2 << 20),
        name="first",
    )(start)
    row_shape = row_blocks[0].shape
    upstream, vector_rows = pl.pallas_call(
        last_kernel,
        grid=(1,),
        in_specs=[
            pl.BlockSpec(memory_space=pltpu.SMEM), pl.BlockSpec(memory_space=pl.ANY), whole(length, group_width)
        ]
        + [whole(*row_shape)] * places,
        out_specs=[
            pl.BlockSpec((length, group_width), lambda i: (0, groups - 1)), whole(row_shape[0], row_shape[1] * places)
        ],
        out_shape=[sds((length, width), BF16), sds((row_shape[0], row_shape[1] * places), F32)],
        input_output_aliases={1: 0},
        compiler_params=params(),
        name="last",
    )(me, buffer, ups[-1], *got)
    return upstream[None], grad_delta.T[None], vector_rows[None], param_sums[None]


def solution(mesh):
    in_specs = (
        P("section", "ctx", "tp"),
        P("section", "ctx", "tp"),
        P("section", "ctx", "tp"),
        P("section", "ctx", "tp"),
        P("section", "tp"),
        P("section", "tp"),
        P("section", "tp"),
        P("section", "ctx", "tp"),
    )
    out_specs = (
        P("section", "ctx", "tp"),
        P("section", "ctx", "tp"),
        P("section", ("ctx", "tp"), None),
        P("section", None, "tp"),
    )

    return jax.shard_map(shards, mesh=mesh, in_specs=in_specs, out_specs=out_specs, check_vma=False)
```

```python
import functools

import jax
import jax.numpy as jnp
from jax import lax
from jax.experimental import pallas as pl
from jax.experimental.pallas import tpu as pltpu
from jax.sharding import PartitionSpec as P


HEADDIM = 64
STATE = 128
CHUNK = 128
LANES = 128
F32 = jnp.float32
BF16 = jnp.bfloat16
TAIL = 8
WIDE = 1024


def iota(shape, dim):
    return lax.broadcasted_iota(jnp.int32, shape, dim)


def mm(a, b):
    return lax.dot_general(a, b, (((1,), (0,)), ((), ())), preferred_element_type=F32)


def mm_nt(a, b):
    return lax.dot_general(a, b, (((1,), (1,)), ((), ())), preferred_element_type=F32)


def split2(v):
    hi = v.astype(BF16)
    return hi, (v - hi.astype(F32)).astype(BF16)


def split3(v):
    hi = v.astype(BF16)
    rest = v - hi.astype(F32)
    mid = rest.astype(BF16)
    return hi, mid, (rest - mid.astype(F32)).astype(BF16)


def softplus(z):
    u = jnp.exp(-jnp.abs(z))
    small = u * (1.0 - u * (0.5 - u * (1.0 / 3.0 - u * (0.25 - u * 0.2))))
    return jnp.maximum(z, 0.0) + jnp.where(u < 0.03, small, jnp.log(1.0 + u))


def chunk_rows(c):
    return slice(c * CHUNK, (c + 1) * CHUNK)


def fill_expand_base(base_ref, heads):
    row, col = iota(base_ref.shape, 0), iota(base_ref.shape, 1)
    width = base_ref.shape[1] // 2
    kind = (row & (2 * heads - 1)) >= heads
    place = (col & (width - 1)) // HEADDIM
    base_ref[...] = jnp.where(kind == (col >= width), (row & (heads - 1)) - place, -64)


def expand(split, base_ref, first_head):
    hit = jnp.where(base_ref[...] == first_head, 1.0, 0.0).astype(BF16)
    out = mm(split, hit)
    width = out.shape[1] // 2
    return out[:, :width], out[:, width:]


def fill_sum_base(base_ref):
    row, col = iota(base_ref.shape, 0), iota(base_ref.shape, 1)
    base_ref[...] = col - (row & (LANES - 1)) // HEADDIM


def sum_pick(base_ref, column):
    return jnp.where(base_ref[...] == column, 1.0, 0.0).astype(BF16)


def head_sum(product, pick):
    return mm(jnp.concatenate(split2(product), axis=1), pick)


def row_ends(cl, chunks):
    return [cl[(c + 1) * CHUNK - 1 : (c + 1) * CHUNK] for c in range(chunks)]


def running(ends):
    before = [jnp.zeros_like(ends[0])]
    for end in ends:
        before.append(before[-1] + end)
    return before


def as_columns(row_ref, width):
    return jnp.concatenate([jnp.broadcast_to(row_ref[...], (LANES, row_ref.shape[1])).T] * (width // LANES), 1)


def prep_kernel(
    x_ref, dy_ref, w_ref, r_ref, delta_ref, rate_ref, bias_ref,
    pay_ref, low_ref, cs_ref, ct_ref, wt_ref, rt_ref, base_ref, *, steps_per_group
):
    quad = pl.program_id(0)
    length = x_ref.shape[0]
    heads = delta_ref.shape[0]
    chunks = length // CHUNK

    @pl.when(quad == 0)
    def _():
        fill_expand_base(base_ref, heads)
        step = softplus(delta_ref[...] + as_columns(bias_ref, length))
        logs = jnp.maximum(jnp.log(step), -200.0)
        decay = -step * jnp.exp(as_columns(rate_ref, length))
        upto = jnp.where(iota((CHUNK, CHUNK), 0) <= iota((CHUNK, CHUNK), 1), 1.0, 0.0).astype(BF16)
        for c in range(chunks):
            hi, mid, lo = split3(decay[:, chunk_rows(c)])
            cum = mm(hi, upto) + mm(mid, upto) + mm(lo, upto)
            both = jnp.concatenate([cum, cum - logs[:, chunk_rows(c)]], axis=0)
            ct_ref[c] = both
            cs_ref[chunk_rows(c), :] = jnp.concatenate(split3(both.T), axis=1)

    @pl.when(quad % steps_per_group == 0)
    def _():
        wt_ref[...] = w_ref[...].astype(F32).T.astype(BF16)
        rt_ref[...] = r_ref[...].astype(F32).T.astype(BF16)

    cl, ll = expand(cs_ref[...], base_ref, quad * (WIDE // HEADDIM))
    before = running(row_ends(cl, chunks))
    total = before[chunks]
    state = jnp.zeros((STATE, WIDE), F32)
    grad = jnp.zeros((STATE, WIDE), F32)
    for c in range(chunks):
        rows = chunk_rows(c)
        drawn = x_ref[rows].astype(F32) * jnp.exp((total - before[c]) - ll[rows])
        w_t, r_t = wt_ref[:, rows], rt_ref[:, rows]
        state += mm(jnp.concatenate([w_t, w_t], 1), jnp.concatenate(split2(drawn), 0))
        pushed = dy_ref[rows].astype(F32) * jnp.exp(before[c] + cl[rows])
        grad += mm(jnp.concatenate([r_t, r_t], 1), jnp.concatenate(split2(pushed), 0))
    carry = jnp.exp(total)
    carry_hi = carry.astype(BF16).astype(F32)
    picked = jnp.where(iota((TAIL, WIDE), 0) == 0, carry_hi, carry - carry_hi).astype(BF16)
    state_hi, state_lo = split2(state)
    grad = grad.astype(BF16)
    for k in range(WIDE // LANES):
        lanes = slice(k * LANES, (k + 1) * LANES)
        pay_ref[k, :STATE] = state_hi[:, lanes]
        pay_ref[k, STATE : 2 * STATE] = grad[:, lanes]
        pay_ref[k, 2 * STATE :] = picked[:, lanes]
        low_ref[k] = state_lo[:, lanes]


def scan_kernel(in_ref, mark_ref, out_ref):
    places = in_ref.shape[0]

    def run(order):
        total = jnp.zeros((STATE, LANES), F32)
        for c in order:
            out_ref[c] = total.astype(BF16)
            mark = mark_ref[c].astype(F32)
            total = (mark[0:1] + mark[1:2]) * total + in_ref[c].astype(F32)

    @pl.when(pl.program_id(0) == 0)
    def _():
        run(range(places))

    @pl.when(pl.program_id(0) == 1)
    def _():
        run(reversed(range(places)))


def local_kernel(
    x_ref, dy_ref, w_ref, r_ref, wt_ref, rt_ref, cs_ref, ct_ref, skip_ref,
    dxi_ref, vp_ref, dwr_ref, gsk_ref, pushed_ref, tail_ref,
    sc_ref, sct_ref, dsc_ref, states_ref, base_ref, sum_base_ref, *, first_pair, heads
):
    place = pl.program_id(0)
    pair = first_pair + place
    length = x_ref.shape[0]
    chunks = length // CHUNK

    @pl.when(place == 0)
    def _():
        for c in range(chunks):
            rows = chunk_rows(c)
            sc_ref[c] = mm_nt(r_ref[rows], w_ref[rows])
            sct_ref[c] = mm_nt(w_ref[rows], r_ref[rows])
        dsc_ref[...] = jnp.zeros_like(dsc_ref)
        vp_ref[...] = jnp.zeros_like(vp_ref)
        dwr_ref[...] = jnp.zeros_like(dwr_ref)
        gsk_ref[...] = jnp.zeros_like(gsk_ref)
        fill_expand_base(base_ref, heads)
        fill_sum_base(sum_base_ref)

    cl, ll = expand(cs_ref[...], base_ref, 2 * pair)
    pick_push = sum_pick(sum_base_ref, 2 * pair)
    pick_drawn = sum_pick(sum_base_ref, 2 * heads + 2 * pair)
    row, col = iota((CHUNK, CHUNK), 0), iota((CHUNK, CHUNK), 1)
    left = iota((CHUNK, LANES), 1) < HEADDIM
    left_b = jnp.where(left, 1.0, 0.0).astype(BF16)
    right_b = jnp.where(left, 0.0, 1.0).astype(BF16)
    skip_sum = jnp.zeros((1, LANES), F32)
    ends = row_ends(cl, chunks)
    before = running(ends)

    state = None
    for c in range(chunks - 1):
        rows = chunk_rows(c)
        hi, lo = split2(x_ref[rows].astype(F32) * jnp.exp(ends[c] - ll[rows]))
        w_t = wt_ref[:, rows]
        written = mm(jnp.concatenate([w_t, w_t], 1), jnp.concatenate([hi, lo], 0))
        state = written if state is None else jnp.exp(ends[c]) * state + written
        states_ref[c + 1] = state

    grad = None
    for c in reversed(range(chunks)):
        rows = chunk_rows(c)
        x, dy = x_ref[rows], dy_ref[rows]
        xf, dyf = x.astype(F32), dy.astype(F32)
        x_two = jnp.concatenate([x * left_b, x * right_b], axis=0)
        dy_two = jnp.concatenate([dy * left_b, dy * right_b], axis=0)
        gram = mm_nt(dy, x_two)
        mixes, mixes_t = [], []
        total = dsc_ref[c]
        for k in range(2):
            lane = slice(k * HEADDIM, k * HEADDIM + 1)
            log_row = ct_ref[c, pl.ds(heads + 2 * pair + k, 1), :]
            decay = jnp.exp(jnp.where(row >= col, cl[rows, lane] - log_row, -1e30))
            mixes.append((sc_ref[c] * decay).astype(BF16))
            total = total + gram[:, k * CHUNK : (k + 1) * CHUNK] * decay
            cum_row = ct_ref[c, pl.ds(2 * pair + k, 1), :]
            decay_t = jnp.exp(jnp.where(col >= row, cum_row - ll[rows, lane], -1e30))
            mixes_t.append((sct_ref[c] * decay_t).astype(BF16))
        dsc_ref[c] = total
        y = mm(jnp.concatenate(mixes, axis=1), x_two)
        dx = mm(jnp.concatenate(mixes_t, axis=1), dy_two)
        seen = jnp.exp(cl[rows])
        pulled_y = dyf * seen
        if c > 0:
            r = r_ref[rows]
            s_hi, s_lo = split2(states_ref[c])
            y = y + seen * mm(jnp.concatenate([r, r], 1), jnp.concatenate([s_hi, s_lo], 0))
            d_hi, d_lo = split2(pulled_y)
            dwr_ref[rows, STATE:] += mm_nt(d_hi, s_hi)
        if grad is not None:
            w = w_ref[rows]
            tail = jnp.exp(ends[c] - ll[rows])
            g_hi, g_lo = split2(grad)
            dx = dx + tail * mm(jnp.concatenate([w, w], 1), jnp.concatenate([g_hi, g_lo], 0))
            dwr_ref[rows, :STATE] += mm_nt((xf * tail).astype(BF16), g_hi)
        if c > 0:
            r_t = rt_ref[:, rows]
            pulled = mm(jnp.concatenate([r_t, r_t], 1), jnp.concatenate([d_hi, d_lo], 0))
            grad = pulled if grad is None else jnp.exp(ends[c]) * grad + pulled
        drawn = xf * dx
        vp_ref[rows] += head_sum(dyf * y - drawn, pick_push) + head_sum(drawn, pick_drawn)
        dxi_ref[0, rows] = dx + skip_ref[...] * dyf
        skip_sum = skip_sum + jnp.sum(xf * dyf, axis=0, keepdims=True)
        pushed_ref[0, rows] = jnp.concatenate(split2(dyf * jnp.exp(before[c] + cl[rows])), 1)
        tail = jnp.exp((before[chunks] - before[c]) - ll[rows])
        tail_ref[0, rows] = tail
    gsk_ref[...] += head_sum(jnp.broadcast_to(skip_sum, (gsk_ref.shape[0], LANES)), pick_push)

    @pl.when(place == pl.num_programs(0) - 1)
    def _():
        for c in range(chunks):
            rows = chunk_rows(c)
            w, r = w_ref[rows], r_ref[rows]
            total = dsc_ref[c]
            hi, lo = split2(total)
            dwr_ref[rows, STATE:] += mm(jnp.concatenate([hi, lo], 1), jnp.concatenate([w, w], 0))
            hi, lo = split2(total.T)
            dwr_ref[rows, :STATE] += mm(jnp.concatenate([hi, lo], 1), jnp.concatenate([r, r], 0))


def inter_kernel(
    me_ref, pushed_ref, tail_ref, x_ref, w_ref, r_ref, pay_ref, low_ref, st_ref, dxi_ref, vp_in_ref, dwr_in_ref,
    gsk_ref, delta_ref, rate_ref, bias_ref, *refs, first_pair, heads, copies, places
):
    *refs, vp_ref, sum_ref, sum_base_ref = refs
    if first_pair:
        gd_in_ref, prm_in_ref, rows_in_ref, *refs = refs
    up_ref, gd_ref, prm_ref, *rows_refs = refs
    place = pl.program_id(0)
    batch, length = pushed_ref.shape[:2]

    @pl.when(place == 0)
    def _():
        vp_ref[...] = vp_in_ref[...]
        sum_ref[...] = dwr_in_ref[...]
        fill_sum_base(sum_base_ref)

    sums = None
    drawn_parts, pushed_parts, grads, states = [], [], [], []
    for k in range(batch):
        pair = first_pair + place * batch + k
        lanes = slice(k * LANES, (k + 1) * LANES)
        state, grad = st_ref[k, :STATE], st_ref[k, STATE:]
        mark = pay_ref[k, 2 * STATE :].astype(F32)
        own = pay_ref[k, :STATE].astype(F32) + low_ref[k].astype(F32)
        ending = own + (mark[0:1] + mark[1:2]) * state.astype(F32)
        edge = jnp.sum(ending * grad.astype(F32), axis=0, keepdims=True)
        pushed, tail = pushed_ref[k], tail_ref[k]
        drawn = x_ref[:, lanes].astype(F32) * tail
        y = mm(r_ref[...], state)
        dx = mm(w_ref[...], grad)
        pulled = drawn * dx
        push = (pushed[:, :LANES].astype(F32) + pushed[:, LANES:].astype(F32)) * y - pulled
        push = push + jnp.where(iota((length, LANES), 0) == length - 1, edge, 0.0)
        found = head_sum(push, sum_pick(sum_base_ref, 2 * pair))
        found = found + head_sum(pulled, sum_pick(sum_base_ref, 2 * heads + 2 * pair))
        sums = found if sums is None else sums + found
        up_ref[:, lanes] = (dxi_ref[k] + tail * dx).astype(BF16)
        drawn_parts += split2(drawn)
        pushed_parts.append(pushed)
        grads += [grad, grad]
        states += [state, state]
    vp_ref[...] += sums
    sum_ref[:, :STATE] += mm_nt(jnp.concatenate(drawn_parts, 1), jnp.concatenate(grads, 1))
    sum_ref[:, STATE:] += mm_nt(jnp.concatenate(pushed_parts, 1), jnp.concatenate(states, 1))

    @pl.when(place == pl.num_programs(0) - 1)
    def _():
        rate = jnp.exp(as_columns(rate_ref, CHUNK))
        bias = as_columns(bias_ref, CHUNK)
        after = jnp.where(iota((CHUNK, CHUNK), 0) >= iota((CHUNK, CHUNK), 1), 1.0, 0.0).astype(BF16)
        rate_sum = jnp.zeros((heads, CHUNK), F32)
        bias_sum = jnp.zeros((heads, CHUNK), F32)
        beyond = jnp.zeros((heads, 1), F32)
        for c in reversed(range(length // CHUNK)):
            rows = chunk_rows(c)
            vp = vp_ref[rows].T
            hi, mid, lo = split3(vp[:heads])
            later = mm(hi, after) + mm(mid, after) + mm(lo, after) + beyond
            beyond = later[:, 0:1]
            z = delta_ref[:, rows] + bias
            step = softplus(z)
            gate = 1.0 / (1.0 + jnp.exp(-z))
            ratio = jnp.where(step < 1e-30, 1.0, gate / jnp.maximum(step, 1e-30))
            grad_delta = vp[2 * heads : 3 * heads] * ratio - rate * later * gate
            rate_sum = rate_sum - rate * later * step
            bias_sum = bias_sum + grad_delta
            if first_pair:
                grad_delta = grad_delta + gd_in_ref[:, rows]
            gd_ref[:, rows] = grad_delta
        lane = iota((heads, LANES), 1)
        rate_sum = jnp.sum(rate_sum, axis=1, keepdims=True)
        bias_sum = jnp.sum(bias_sum, axis=1, keepdims=True)
        both = jnp.where(lane == 0, rate_sum, jnp.where(lane == 1, bias_sum, 0.0))
        both = jnp.concatenate([both, jnp.zeros((LANES - heads, LANES), F32)], 0).T[:8]
        sums = jnp.where(iota((8, LANES), 0) == 2, gsk_ref[...], both)
        if first_pair:
            sums = sums + prm_in_ref[0]
        for k in range(copies):
            prm_ref[k] = sums
        rows = length // len(rows_refs)
        for hop, ref in enumerate(rows_refs):
            start = pl.multiple_of(lax.rem(me_ref[0] + hop, places) * rows, rows) if len(rows_refs) > 1 else 0
            if first_pair:
                ref[:, : -2 * STATE] = rows_in_ref[pl.ds(start, rows), :]
            ref[:, -2 * STATE :] = sum_ref[pl.ds(start, rows), :].astype(BF16)


def first_kernel(in_ref, out_ref):
    out_ref[...] = in_ref[...]


def last_kernel(me_ref, buffer_ref, up_ref, *refs):
    *in_refs, all_ref, out_ref = refs
    all_ref[...] = up_ref[...]
    places = len(in_refs)
    width = in_refs[0].shape[1]
    for hop, ref in enumerate(in_refs):
        source = lax.rem(me_ref[0] + (places - hop), places)
        out_ref[:, pl.ds(pl.multiple_of(source * width, width), width)] = ref[...].astype(F32)


def params():
    return pltpu.CompilerParams(dimension_semantics=("arbitrary",), vmem_limit_bytes=67043328)


def cost(flops, moved):
    return pl.CostEstimate(flops=flops, bytes_accessed=moved, transcendentals=0)


def whole(*shape):
    return pl.BlockSpec(shape, lambda *ids: (0,) * len(shape))


def shards(
    mixer_input, write_vectors, read_vectors, delta_raw, log_rates, delta_bias, skip_gain, output_grad
):
    length, width = mixer_input.shape[1:]
    heads = delta_raw.shape[2]
    groups = write_vectors.shape[2] // STATE
    pairs = width // LANES
    per_group = pairs // groups
    group_width = width // groups
    depth = 6 * heads
    sds = jax.ShapeDtypeStruct
    x, dy = mixer_input[0], output_grad[0]
    w, r, delta = write_vectors[0], read_vectors[0], delta_raw[0].T

    steps = width // WIDE
    steps_per_group = steps // groups
    col = pl.BlockSpec((length, WIDE), lambda j: (0, j))
    grp = pl.BlockSpec((length, STATE), lambda j: (0, j // steps_per_group))
    grp_t = pl.BlockSpec((STATE, length), lambda j: (j // steps_per_group, 0))
    pay_rows = 2 * STATE + TAIL
    pay, low, cs, ct, wt, rt = pl.pallas_call(
        functools.partial(prep_kernel, steps_per_group=steps_per_group),
        grid=(steps,),
        in_specs=[col, col, grp, grp, whole(heads, length), whole(1, heads), whole(1, heads)],
        out_specs=[
            pl.BlockSpec((WIDE // LANES, pay_rows, LANES), lambda j: (j, 0, 0)),
            pl.BlockSpec((WIDE // LANES, STATE, LANES), lambda j: (j, 0, 0)),
            whole(length, depth),
            whole(length // CHUNK, 2 * heads, CHUNK),
            grp_t,
            grp_t,
        ],
        out_shape=[
            sds((pairs, pay_rows, LANES), BF16),
            sds((pairs, STATE, LANES), BF16),
            sds((length, depth), BF16),
            sds((length // CHUNK, 2 * heads, CHUNK), F32),
            sds((groups * STATE, length), BF16),
            sds((groups * STATE, length), BF16),
        ],
        scratch_shapes=[pltpu.VMEM((depth, 2 * WIDE), jnp.int32)],
        compiler_params=params(),
        name="prep",
    )(x, dy, w, r, delta, log_rates, delta_bias)

    skip_row = jnp.repeat(skip_gain, HEADDIM, axis=1)
    own_col = pl.BlockSpec((1, length, LANES), lambda p: (p, 0, 0))
    own_two = pl.BlockSpec((1, length, 2 * LANES), lambda p: (p, 0, 0))
    batch = 2
    trips = per_group // batch

    def many(*shape):
        return pl.BlockSpec((batch, *shape), lambda p: (p, 0, 0))

    def many_of(g, *shape):
        return pl.BlockSpec((batch, *shape), lambda p: (g * trips + p, 0, 0))

    me = lax.axis_index("tp")[None]
    places, copies = lax.axis_size("tp"), lax.axis_size("ctx")

    def group_specs(g):
        first = g * per_group
        col_g = pl.BlockSpec((length, LANES), lambda p: (0, first + p))
        grp_g = pl.BlockSpec((length, STATE), lambda p: (0, g))
        grp_tg = pl.BlockSpec((STATE, length), lambda p: (g, 0))
        return first, col_g, grp_g, grp_tg

    def local(g, cs):
        first, col_g, grp_g, grp_tg = group_specs(g)
        return pl.pallas_call(
            functools.partial(local_kernel, first_pair=first, heads=heads),
            grid=(per_group,),
            in_specs=[
                col_g, col_g, grp_g, grp_g, grp_tg, grp_tg, whole(length, depth),
                whole(length // CHUNK, 2 * heads, CHUNK),
                pl.BlockSpec((1, LANES), lambda p: (0, first + p)),
            ],
            out_specs=[
                own_col, whole(length, LANES), whole(length, 2 * STATE), whole(8, LANES), own_two, own_col
            ],
            out_shape=[
                sds((per_group, length, LANES), F32),
                sds((length, LANES), F32),
                sds((length, 2 * STATE), F32),
                sds((8, LANES), F32),
                sds((per_group, length, 2 * LANES), BF16),
                sds((per_group, length, LANES), F32),
            ],
            scratch_shapes=[pltpu.VMEM((length // CHUNK, CHUNK, CHUNK), F32)] * 4
            + [pltpu.VMEM((depth, 2 * LANES), jnp.int32), pltpu.VMEM((2 * LANES, LANES), jnp.int32)],
            compiler_params=params(),
            cost_estimate=cost(20 * 10**9, 64 << 20),
            name="local",
        )(x, dy, w, r, wt, rt, cs, ct, skip_row)

    def inter(g, edges, own, carried):
        first, _, grp_g, _ = group_specs(g)
        dxi, vp, dwr, gsk, pushed, tail = own
        final = g == groups - 1
        mine = copies if final else 1
        row_width = 2 * STATE * (g + 1)
        row_shapes = [(length // places, row_width)] * places if final else [(length, row_width)]
        return pl.pallas_call(
            functools.partial(inter_kernel, first_pair=first, heads=heads, copies=mine, places=places),
            grid=(trips,),
            in_specs=[
                pl.BlockSpec(memory_space=pltpu.SMEM),
                many(length, 2 * LANES), many(length, LANES),
                pl.BlockSpec((length, batch * LANES), lambda p: (0, g * trips + p)), grp_g, grp_g,
                many_of(g, pay_rows, LANES), many_of(g, STATE, LANES), many_of(g, 2 * STATE, LANES),
                many(length, LANES), whole(length, LANES), whole(length, 2 * STATE), whole(8, LANES),
                whole(heads, length), whole(1, heads), whole(1, heads), *[whole(*a.shape) for a in carried],
            ],
            out_specs=[
                pl.BlockSpec((length, batch * LANES), lambda p: (0, p)), whole(heads, length), whole(mine, 8, LANES),
                *[whole(*shape) for shape in row_shapes],
            ],
            out_shape=[
                sds((length, group_width), BF16), sds((heads, length), F32), sds((mine, 8, LANES), F32),
                *[sds(shape, BF16) for shape in row_shapes],
            ],
            scratch_shapes=[
                pltpu.VMEM((length, LANES), F32),
                pltpu.VMEM((length, 2 * STATE), F32),
                pltpu.VMEM((2 * LANES, LANES), jnp.int32),
            ],
            compiler_params=params(),
            cost_estimate=cost(4 * 10**9, 16 << 20),
            name="inter",
        )(me, pushed, tail, x, w, r, pay, low, edges, dxi, vp, dwr, gsk, delta, log_rates, delta_bias, *carried)

    arrived = lax.all_to_all(pay, "ctx", split_axis=0, concat_axis=0, tiled=True)
    own = [local(0, cs)]
    arrived, own[0] = lax.optimization_barrier((arrived, own[0]))
    scanned = pl.pallas_call(
        scan_kernel,
        in_specs=[
            pl.BlockSpec((pairs, STATE, LANES), lambda i: (0, i, 0)),
            pl.BlockSpec((pairs, TAIL, LANES), lambda i: (0, 2 * STATE // TAIL, 0)),
        ],
        out_specs=pl.BlockSpec((pairs, STATE, LANES), lambda i: (0, i, 0)),
        out_shape=sds((pairs, 2 * STATE, LANES), BF16),
        compiler_params=params(),
        grid=(2,),
        name="scan",
    )(arrived, arrived)
    scanned, cs_later = lax.optimization_barrier((scanned, cs))
    edges = lax.all_to_all(scanned, "ctx", split_axis=0, concat_axis=0, tiled=True)
    own += [local(g, cs_later) for g in range(1, groups)]
    edges, own = lax.optimization_barrier((edges, own))

    devices = range(lax.axis_size("section"))
    route = [(i + 1, i) for i in devices if i + 1 in devices]
    ups, carried = [], []
    for g in range(groups):
        up, *carried = inter(g, edges, own[g], carried)
        ups.append(lax.ppermute(up, "section", route))
    grad_delta, sums, *row_blocks = carried
    everyone = lax.all_to_all(sums, "ctx", split_axis=0, concat_axis=0, tiled=True)
    got = row_blocks[:1]
    for hop in range(1, places):
        got.append(lax.ppermute(row_blocks[hop], "tp", [(i, (i + hop) % places) for i in range(places)]))
    param_sums = jnp.sum(everyone, axis=0)[:3, :heads]
    before = width - group_width
    start = jnp.concatenate(ups[:-1], axis=1) if groups > 2 else ups[0]
    buffer = pl.pallas_call(
        first_kernel,
        grid=(1,),
        in_specs=[whole(length, before)],
        out_specs=whole(length, before),
        out_shape=sds((length, width), BF16),
        compiler_params=params(),
        cost_estimate=cost(10**6, 2 << 20),
        name="first",
    )(start)
    row_shape = row_blocks[0].shape
    upstream, vector_rows = pl.pallas_call(
        last_kernel,
        grid=(1,),
        in_specs=[
            pl.BlockSpec(memory_space=pltpu.SMEM), pl.BlockSpec(memory_space=pl.ANY), whole(length, group_width)
        ]
        + [whole(*row_shape)] * places,
        out_specs=[
            pl.BlockSpec((length, group_width), lambda i: (0, groups - 1)), whole(row_shape[0], row_shape[1] * places)
        ],
        out_shape=[sds((length, width), BF16), sds((row_shape[0], row_shape[1] * places), F32)],
        input_output_aliases={1: 0},
        compiler_params=params(),
        name="last",
    )(me, buffer, ups[-1], *got)
    return upstream[None], grad_delta.T[None], vector_rows[None], param_sums[None]


def solution(mesh):
    in_specs = (
        P("section", "ctx", "tp"),
        P("section", "ctx", "tp"),
        P("section", "ctx", "tp"),
        P("section", "ctx", "tp"),
        P("section", "tp"),
        P("section", "tp"),
        P("section", "tp"),
        P("section", "ctx", "tp"),
    )
    out_specs = (
        P("section", "ctx", "tp"),
        P("section", "ctx", "tp"),
        P("section", ("ctx", "tp"), None),
        P("section", None, "tp"),
    )

    return jax.shard_map(shards, mesh=mesh, in_specs=in_specs, out_specs=out_specs, check_vma=False)
```
